32 devices in a mesh: cols: 4 (over y, core), levs: 2 (over x), owner: 4 (over z).
Axes of the slice: x: 2, y: 2, z: 4, core: 2. Of those that a mesh axis runs over, the one named last changes fastest.
Arguments:
- perturbations: bfloat16 [80, 32, 4096], P(None, 'levs', 'cols'), may hold values from -8 to 8
- background: float32 [32, 4096], P('levs', 'cols'), may hold values from -6 to 6
- obs_cols: int32 [4, 2048], P(None, 'owner'), may hold values from 0 to 4095, as said below
- obs_levs: int32 [4, 2048], P(None, 'owner'), may hold values from 0 to 31
- obs_vals: float32 [4, 2048], P(None, 'owner'), may hold values from -12 to 12
- obs_sigma: float32 [4, 2048], P(None, 'owner'), may hold values from 2 to 4
- pairs: int32 [4, 32, 16], P(None, 'cols'), may hold values 0 or 1
Outputs:
- analysis_mean: float32 [32, 4096], P('levs', 'cols')
- analysis_pert: bfloat16 [80, 32, 4096], P(None, 'levs', 'cols')
The draws below stay inside these ranges and needn't reach their ends.
Inputs may be any that keep to these rules, and one draw needn't show every extreme that they name: `obs_cols`: for each batch, the 512 observations held by one owner index fall in the columns of one cols index (a run of 1024 columns) at most 384 times, and exactly 384 times for some cols index.
All inputs are finite; a program needn't handle non-finite values. No bound on the sum of `pairs` on one device may be relied on, other than what follows from the above.
Results may differ from the reference program's by a relative error of at most 0.0088.
Values sent between devices are 32-bit elements; how exact they have to be, the bound alone decides.
No kernel may reach another device: no remote copies, remote signals or barrier semaphores. Data moves between devices by JAX's collectives and lax.ppermute only.
A program may use at most 64 MiB of HBM per device.

```python
import math
import jax
import jax.numpy as jnp
from jax import lax

MEMBERS = 80
TILE_COLS = 128
OBLK = 128
BATCHES = 4
OBS_OWN = 512
COL_DEV = 1024
COLS = 4096
TILES = 32
LEVS = 32
OBS = 2048
NBLK = 16
N_COLS = 4
N_OWNER = 4


def draw_obs_cols(key, part):
    capacity = min(OBS_OWN, 3 * OBS_OWN // N_COLS)
    spread = max(N_COLS - 1, 1)

    def one_share(subkey):
        key_busy, key_order, key_offset = jax.random.split(subkey, 3)
        busiest = jax.random.randint(key_busy, (), 0, N_COLS)
        position = jnp.arange(OBS_OWN, dtype=jnp.int32)
        remaining = jnp.maximum(position - capacity, 0)
        others = (busiest + 1 + jnp.mod(remaining, spread)) % N_COLS
        target = jnp.where(position < capacity, busiest, others)
        target = jax.random.permutation(key_order, target)
        offset = jax.random.randint(key_offset, (OBS_OWN,), 0, COL_DEV)
        return (target * COL_DEV + offset).astype(jnp.int32)
    subkeys = jax.random.split(jax.random.fold_in(key, 7), BATCHES * N_OWNER)
    return jax.vmap(one_share)(subkeys).reshape(BATCHES, N_OWNER * OBS_OWN)


def draw_perturbations(key, part):
    base = jax.random.fold_in(key, 11)
    key_noise, key_member, key_cell = jax.random.split(base, 3)
    noise = jax.random.normal(key_noise, (MEMBERS, LEVS, COLS), jnp.float32)
    member_part = jax.random.normal(key_member, (MEMBERS, 1, 1), jnp.float32)
    cell_part = jax.random.normal(key_cell, (1, LEVS, COLS), jnp.float32)
    total = noise + member_part * cell_part
    return jnp.clip(total, -8.0, 8.0).astype(jnp.bfloat16)


def set_ends(array, own_key, smallest, top_value):
    extent = array.shape
    spot = [jax.random.randint(jax.random.fold_in(own_key, axis), (), 0, extent[axis]) for axis in range(len(extent))]
    array = array.at[tuple(spot)].set(smallest)
    longest = extent.index(max(extent))
    spot[longest] = (spot[longest] + 1) % extent[longest]
    return array.at[tuple(spot)].set(top_value)


def steps_of(own_key, shape, pieces, smallest, high):
    factor_of, own = 1.0, jax.random.fold_in(own_key, 6)
    for dim, parts in pieces:
        steps = jnp.exp(jax.random.uniform(jax.random.fold_in(own, dim), (parts,), jnp.float32, smallest / len(pieces), high / len(pieces)))
        factor_of = factor_of * jnp.repeat(steps, shape[dim] // parts).reshape([-1 if axis == dim else 1 for axis in range(len(shape))])
    return factor_of


def gaussian(key, extent, deviation, reach, pieces=(), held_as=jnp.bfloat16):
    values = deviation * jax.random.normal(key, extent, jnp.float32)
    if pieces:
        values = values * steps_of(key, extent, pieces, -0.22, 0.18)
    return jnp.clip(values, -reach, reach).astype(held_as)


def setup_inputs(seed: int = 0) -> dict:
    key_of = jax.random.split(jax.random.key(seed), 8)
    return {
        "perturbations": draw_perturbations(jax.random.fold_in(key_of[7], 71), 0),
        "background": gaussian(key_of[1], (LEVS, COLS), 1.0, 6.0, ((0, 2), (1, 4)), jnp.float32),
        "obs_cols": draw_obs_cols(jax.random.fold_in(key_of[7], 71), 0),
        "obs_levs": set_ends(jax.random.randint(key_of[3], (BATCHES, OBS), 0, LEVS), jax.random.fold_in(key_of[3], 1), 0, LEVS - 1).astype(jnp.int32),
        "obs_vals": gaussian(key_of[4], (BATCHES, OBS), 3.0, 12.0, ((1, 4),), jnp.float32),
        "obs_sigma": jnp.clip(jnp.exp(math.log(4.0) - 0.6931472 * jax.random.uniform(key_of[5], (BATCHES, OBS), jnp.float32) ** steps_of(key_of[5], (BATCHES, OBS), ((1, 4),), -0.2, 0.2)), 2.0, 4.0),
        "pairs": set_ends((jax.random.randint(key_of[6], (BATCHES, TILES, NBLK), 0, 2) < 1).astype(jnp.int32), jax.random.fold_in(key_of[6], 1), 0, 1),
    }


def reference(perturbations, background, obs_cols, obs_levs, obs_vals, obs_sigma, pairs):
    root_value = math.sqrt(MEMBERS - 1.0)
    highest = lax.Precision.HIGHEST
    identity = jnp.eye(MEMBERS, dtype=jnp.float32)
    pert = perturbations
    mean = background
    for batch_index in range(BATCHES):
        cols_now = obs_cols[batch_index].astype(jnp.int32)
        levs_now = obs_levs[batch_index].astype(jnp.int32)
        sigma = obs_sigma[batch_index]
        observed = pert[:, levs_now, cols_now].astype(jnp.float32)
        observed_mean = mean[levs_now, cols_now]
        weight_scale = 1.0 / (sigma * root_value)
        scaled = observed * weight_scale[None, :]
        innov = (obs_vals[batch_index] - observed_mean) / sigma
        blocks = scaled.reshape(MEMBERS, NBLK, OBLK)
        gram = jnp.einsum('mbo,nbo->bmn', blocks, blocks, precision=highest)
        cross = jnp.einsum('mbo,bo->bm', blocks, innov.reshape(NBLK, OBLK), precision=highest)
        pair_float = pairs[batch_index].astype(jnp.float32)
        system = identity[None] + jnp.einsum('tb,bmn->tmn', pair_float, gram, precision=highest)
        forcing = jnp.einsum('tb,bm->tm', pair_float, cross, precision=highest)
        factor = jnp.linalg.cholesky(system)
        inverse = lax.linalg.triangular_solve(factor, jnp.broadcast_to(identity, system.shape), left_side=True, lower=True)
        transform = jnp.swapaxes(inverse, 1, 2)
        halfway = jnp.einsum('tmn,tn->tm', inverse, forcing, precision=highest)
        weights = jnp.einsum('tmn,tn->tm', transform, halfway, precision=highest).astype(jnp.bfloat16)
        transform_b = transform.astype(jnp.bfloat16)
        tile_view = pert.reshape(MEMBERS, LEVS, TILES, TILE_COLS).astype(jnp.float32)
        increment = jnp.einsum('mltc,tm->ltc', tile_view, weights.astype(jnp.float32)) / root_value
        updated = jnp.einsum('mltc,tmn->nltc', tile_view, transform_b.astype(jnp.float32))
        mean = mean + increment.reshape(LEVS, COLS)
        pert = updated.astype(jnp.bfloat16).reshape(MEMBERS, LEVS, COLS)
    return (mean, pert)
```

```python
import functools
import math

import jax
import jax.numpy as jnp
from jax import lax
from jax.experimental import pallas as pl
from jax.experimental.pallas import tpu as pltpu
from jax.sharding import PartitionSpec as P

F32 = jnp.float32
BF16 = jnp.bfloat16
LANES = 128
GROUP = 8
DROWS = 96
VMEM_BYTES = 40 << 20


def params():
    return pltpu.CompilerParams(vmem_limit_bytes=VMEM_BYTES)


def split2(x):
    high = x.astype(BF16)
    return high, (x - high.astype(F32)).astype(BF16)


def nt_dot(a, b):
    return lax.dot_general(a, b, (((1,), (1,)), ((), ())), preferred_element_type=F32)


def observe_into(y_ref, hot_ref, pert_ref, mean_ref, local_cols, local_levs):
    col_dev, count = hot_ref.shape
    lev_dev = mean_ref.shape[0]
    members = pert_ref.shape[0] // lev_dev
    for start in range(0, col_dev, 256):
        rows = lax.broadcasted_iota(jnp.int32, (256, count), 0) + start
        hot_ref[start : start + 256, :] = jnp.where(rows == local_cols, 1.0, 0.0).astype(BF16)
    lev_hot = lax.broadcasted_iota(jnp.int32, (lev_dev, count), 0) == local_levs
    hot = hot_ref[...]
    step = 16
    for start in range(0, members, step):
        picked = jnp.dot(
            pert_ref[start * lev_dev : (start + step) * lev_dev, :], hot, preferred_element_type=F32
        ).reshape(step, lev_dev, count)
        y_ref[start : start + step, :] = jnp.sum(jnp.where(lev_hot[None], picked, 0.0), axis=1)
    mean = mean_ref[...]
    high = mean.astype(BF16)
    rest = mean - high.astype(F32)
    middle = rest.astype(BF16)
    low = (rest - middle.astype(F32)).astype(BF16)
    picked = jnp.dot(jnp.concatenate([high, middle, low], axis=0), hot, preferred_element_type=F32)
    picked = (
        picked[:lev_dev] + picked[lev_dev : 2 * lev_dev] + picked[2 * lev_dev : 3 * lev_dev]
    )
    total = jnp.sum(jnp.where(lev_hot, picked, 0.0), axis=0, keepdims=True)
    tail = y_ref.shape[0] - members
    first = lax.broadcasted_iota(jnp.int32, (tail, count), 0) == 0
    y_ref[members:, :] = jnp.where(first, jnp.broadcast_to(total, (tail, count)), 0.0)


def block_grams(values, mean_row, sigma, vals, members, store):
    root = math.sqrt(members - 1.0)
    count = values.shape[1]
    scale = 1.0 / (sigma * root)
    innov = (vals - mean_row) / sigma
    wide = values.astype(F32) * (scale * scale)
    pad = LANES - members
    first = lax.broadcasted_iota(jnp.int32, (pad, count), 0) == 0
    last = jnp.where(first, jnp.broadcast_to(scale * innov, (pad, count)), 0.0)
    high, low = split2(jnp.concatenate([wide, last], axis=0))
    for block in range(count // LANES):
        at = slice(block * LANES, (block + 1) * LANES)
        left = jnp.concatenate([values[:, at], values[:, at]], axis=1)
        right = jnp.concatenate([high[:, at], low[:, at]], axis=1)
        store(block, nt_dot(left, right))


def first_kernel(pert_ref, mean_ref, cols_ref, levs_ref, sigma_ref, vals_ref, keep_ref, send_ref, y_ref, hot_ref):
    observe_into(y_ref, hot_ref, pert_ref, mean_ref, cols_ref[...], levs_ref[...])
    members = keep_ref.shape[1]
    own_blocks = keep_ref.shape[0]

    def store(block, product):
        if block < own_blocks:
            keep_ref[block] = product
        else:
            send_ref[block - own_blocks] = product

    block_grams(
        y_ref[:members, :].astype(BF16), y_ref[members : members + 1, :], sigma_ref[...], vals_ref[...], members, store
    )


def observe_kernel(pert_ref, mean_ref, cols_ref, levs_ref, keep_ref, send_ref, y_ref, hot_ref):
    observe_into(y_ref, hot_ref, pert_ref, mean_ref, cols_ref[0], levs_ref[0])
    half = keep_ref.shape[2]
    keep_ref[0] = y_ref[:, :half]
    send_ref[0] = y_ref[:, half:]


def build_systems(m_ref, pair_ref, order_ref, own_ref, peer_ref):
    tiles = pair_ref.shape[0]
    members = own_ref.shape[1]
    spread = jnp.dot(pair_ref[...].astype(BF16), order_ref[...], preferred_element_type=F32)
    lane = lax.broadcasted_iota(jnp.int32, (tiles, spread.shape[1]), 1)
    select = jnp.concatenate(
        [jnp.where(lane % GROUP == row, spread, 0.0) for row in range(GROUP)], axis=0
    ).astype(BF16)
    out_lane = lax.broadcasted_iota(jnp.int32, (tiles, LANES), 1)
    for start in range(0, members, GROUP):
        at = slice(start, start + GROUP)
        stacked = jnp.concatenate(
            [ref[block, at, :] for ref in (own_ref, peer_ref) for block in range(ref.shape[0])], axis=0
        )
        high, low = split2(stacked)
        product = jnp.dot(select, jnp.concatenate([high, low], axis=0), preferred_element_type=F32)
        for row in range(GROUP):
            part = product[row * tiles : (row + 1) * tiles]
            m_ref[(start + row) * tiles : (start + row + 1) * tiles, :] = part + jnp.where(
                out_lane == start + row, 1.0, 0.0
            )


def invert_factors(m_ref, w_ref, members):
    tiles = w_ref.shape[0]
    chunk = min(tiles, 32)
    lane = lax.broadcasted_iota(jnp.int32, (chunk, LANES), 1)

    def one_chunk(base):
        def row_at(row):
            return m_ref.at[pl.ds(row * tiles + base, chunk), :]

        weights = jnp.zeros((chunk, LANES), F32)
        for start in range(0, members, GROUP):
            upper = [row_at(start + a)[...] for a in range(GROUP)]
            pivots = []
            for a in range(GROUP):
                pivot = jnp.broadcast_to(upper[a][:, start + a : start + a + 1], (chunk, LANES))
                inverse = 1.0 / pivot
                pivots.append((pivot, inverse))
                scaled = jnp.where(lane == start + a, 1.0 + inverse, upper[a] * inverse)
                for b in range(a + 1, GROUP):
                    upper[b] = upper[b] - upper[b][:, start + a : start + a + 1] * scaled
            lower = [
                jnp.where(
                    lane == start + a,
                    1.0,
                    jnp.where((lane > start + a) & (lane < start + GROUP), 0.0, upper[a]),
                )
                for a in range(GROUP)
            ]
            if start + GROUP < members:
                solved = [None] * GROUP
                for a in range(GROUP - 1, -1, -1):
                    total = lower[a]
                    for b in range(a + 1, GROUP):
                        total = total - upper[a][:, start + b : start + b + 1] * solved[b]
                    solved[a] = total * pivots[a][1]
                solved = [jnp.where(lane == start + a, solved[a] + 1.0, solved[a]) for a in range(GROUP)]
            for a in range(GROUP):
                row = lower[a] * lax.rsqrt(pivots[a][0])
                halfway = row[:, members : members + 1]
                row = jnp.where(lane <= start + a, row, 0.0)
                weights = weights + halfway * row
                row_at(start + a)[...] = row
            if start + GROUP < members:

                def trailing(index, carry, start=start, solved=solved):
                    first = start + GROUP + index * GROUP
                    for low in range(0, chunk, GROUP):
                        for a in range(GROUP):
                            at = m_ref.at[pl.ds((first + a) * tiles + base + low, GROUP), :]
                            row = at[...]
                            new = row
                            for b in range(GROUP):
                                new = new - row[:, start + b : start + b + 1] * solved[b][low : low + GROUP]
                            at[...] = new
                    return carry

                lax.fori_loop(0, (members - start - GROUP) // GROUP, trailing, 0)
        w_ref[pl.ds(base, chunk), :] = weights

    if chunk == tiles:
        one_chunk(0)
    else:

        @pl.loop(0, tiles // chunk)
        def _(index):
            one_chunk(pl.multiple_of(index * chunk, chunk))


def product_of(m_ref, w_ref, tile, old, members):
    tiles = w_ref.shape[0]
    rows = m_ref[pl.ds(tile, members, stride=tiles), :].astype(BF16)
    tail = DROWS - members
    sub = lax.broadcasted_iota(jnp.int32, (tail, LANES), 0)
    lane = lax.broadcasted_iota(jnp.int32, (tail, LANES), 1)
    weights = jnp.broadcast_to(w_ref[pl.ds(tile, 1), :], (tail, LANES)).astype(BF16).astype(F32)
    if old is None:
        return jnp.concatenate([rows, jnp.where(sub == 0, weights, 0.0).astype(BF16)], axis=0)
    ones = (lane >= members) & (lane < members + 2)
    extra = jnp.where(sub == 0, jnp.where(ones, 1.0, weights), 0.0).astype(BF16)
    left = jnp.concatenate([rows, extra], axis=0)[:, :DROWS]
    new = jnp.dot(left, old, preferred_element_type=F32)
    total = jnp.broadcast_to(new[members : members + 1, :], (tail, LANES))
    high = total.astype(BF16).astype(F32)
    last = jnp.where(sub == 0, high, jnp.where(sub == 1, total - high, 0.0))
    return jnp.concatenate([new[:members], last], axis=0).astype(BF16)


def products(m_ref, w_ref, old_ref, new_ref, members):
    def pair(index, carry):
        for side in range(2):
            at = slice(side * LANES, (side + 1) * LANES)
            old = None if old_ref is None else old_ref[index, :, at]
            new_ref[index, :, at] = product_of(m_ref, w_ref, index * 2 + side, old, members)
        return carry

    lax.fori_loop(0, new_ref.shape[0], pair, 0, unroll=2)


def batch_kernel(first, *refs):
    if first:
        (pair_ref, order_ref, own_ref, peer_ref, y_ref, tile_ref, sigma_ref, vals_ref, new_ref, gram_ref, m_ref, w_ref, x_ref) = refs
        old_ref = None
    else:
        (pair_ref, order_ref, own_ref, peer_ref, y_ref, tile_ref, sigma_ref, vals_ref, old_ref, new_ref, gram_ref, m_ref, w_ref, x_ref) = refs
    members = own_ref.shape[1]
    root = math.sqrt(members - 1.0)
    build_systems(m_ref, pair_ref, order_ref, own_ref, peer_ref)
    invert_factors(m_ref, w_ref, members)
    products(m_ref, w_ref, old_ref, new_ref, members)
    tile = tile_ref[...]
    count = tile.shape[1]
    start_values = y_ref[:members, :]
    empty = jnp.zeros((LANES - members, count), BF16)
    for side in range(2):
        x_ref[side * LANES : side * LANES + members, :] = jnp.where(tile % 2 == side, start_values, 0.0).astype(BF16)
        x_ref[side * LANES + members : (side + 1) * LANES, :] = empty
    stacked = x_ref[...]
    half_tile = tile // 2
    per = 4

    def gather(index, total):
        at = new_ref[pl.ds(index * per, per)].reshape(per * DROWS, 2 * LANES)
        product = jnp.dot(at, stacked, preferred_element_type=F32)
        for k in range(per):
            total = jnp.where(half_tile == index * per + k, product[k * DROWS : (k + 1) * DROWS], total)
        return total

    now = lax.fori_loop(0, new_ref.shape[0] // per, gather, jnp.zeros((DROWS, count), F32))
    mean_row = y_ref[members : members + 1, :] + (now[members : members + 1] + now[members + 1 : members + 2]) / root

    def store(block, product):
        gram_ref[block] = product

    block_grams(now[:members].astype(BF16), mean_row, sigma_ref[...], vals_ref[...], members, store)


def last_kernel(pair_ref, order_ref, own_ref, peer_ref, old_ref, pert_ref, mean_ref, out_mean_ref, out_ref, m_ref, w_ref, new_ref):
    members = own_ref.shape[1]
    root = math.sqrt(members - 1.0)
    build_systems(m_ref, pair_ref, order_ref, own_ref, peer_ref)
    invert_factors(m_ref, w_ref, members)
    products(m_ref, w_ref, old_ref, new_ref, members)
    tiles = w_ref.shape[0]
    width = pert_ref.shape[2] // tiles
    for tile in range(tiles):
        side = tile % 2
        left = new_ref[tile // 2, :, side * LANES : side * LANES + members]
        at = slice(tile * width, (tile + 1) * width)
        for lev in range(pert_ref.shape[0]):
            new = jnp.dot(left, pert_ref[lev, :, at], preferred_element_type=F32)
            out_ref[lev, :, at] = new[:members].astype(BF16)
            gain = new[members : members + 1] + new[members + 1 : members + 2]
            out_mean_ref[lev : lev + 1, at] = mean_ref[lev : lev + 1, at] + gain / root


def swap(x, axis, bit):
    return lax.ppermute(x, axis, [(i, i ^ bit) for i in range(lax.axis_size(axis))])


def upper_bits(axis, first):
    bit, bits = first, []
    while bit < lax.axis_size(axis):
        bits.append(bit)
        bit *= 2
    return bits


def plane_sum(keep, send):
    total = keep + swap(send, "cols", 1)
    for bit in upper_bits("cols", 2):
        total = total + swap(total, "cols", bit)
    for bit in upper_bits("levs", 1):
        total = total + swap(total, "levs", bit)
    return total


def body(perturbations, background, obs_cols, obs_levs, obs_vals, obs_sigma, pairs):
    members, lev_dev, col_dev = perturbations.shape
    batches, obs_own = obs_cols.shape
    tiles_dev, block_count = pairs.shape[1:]
    tile_cols = col_dev // tiles_dev
    cols_size, owners = lax.axis_size("cols"), lax.axis_size("owner")
    tiles = tiles_dev * cols_size
    own_blocks = block_count // owners // 2
    half = obs_own // 2
    cols_index = lax.axis_index("cols")
    core = cols_index % 2
    owner = lax.axis_index("owner")

    def halves(x):
        parts = x.reshape(batches, 2, half)
        return jnp.where(core == 0, parts, parts[:, ::-1])

    cols_half = halves(obs_cols)
    local_cols = (cols_half - cols_index * col_dev).reshape(batches, 1, obs_own)
    local_levs = (halves(obs_levs) - lax.axis_index("levs") * lev_dev).reshape(batches, 1, obs_own)
    sigma_half = halves(obs_sigma)
    vals_half = halves(obs_vals)
    tile_half = cols_half[:, 0] // tile_cols

    all_pairs = pairs.astype(F32)
    for bit in upper_bits("cols", 1):
        other = swap(all_pairs, "cols", bit)
        upper = (cols_index // bit) % 2 == 1
        all_pairs = jnp.where(
            upper, jnp.concatenate([other, all_pairs], axis=1), jnp.concatenate([all_pairs, other], axis=1)
        )

    place = jnp.arange(2 * block_count * GROUP) // GROUP % block_count
    side, rest = place // (block_count // 2), place % (block_count // 2)
    hop, block = rest // own_blocks, rest % own_blocks
    wanted = (owner ^ hop) * (2 * own_blocks) + (core ^ side) * own_blocks + block
    order = (jnp.arange(block_count)[:, None] == wanted[None, :]).astype(BF16)

    flat = perturbations.reshape(members * lev_dev, col_dev)
    gram = jax.ShapeDtypeStruct((own_blocks, members, LANES), F32)
    observed_scratch = [pltpu.VMEM((88, obs_own), F32), pltpu.VMEM((col_dev, obs_own), BF16)]
    keep, send = pl.pallas_call(
        first_kernel,
        out_shape=(gram, gram),
        scratch_shapes=observed_scratch,
        compiler_params=params(),
        name="first",
    )(
        flat,
        background,
        local_cols[0],
        local_levs[0],
        sigma_half[0].reshape(1, obs_own),
        vals_half[0].reshape(1, obs_own),
    )
    later = jax.ShapeDtypeStruct((batches - 1, 88, half), F32)
    row_spec = pl.BlockSpec((1, 1, obs_own), lambda k: (k, 0, 0))
    out_spec = pl.BlockSpec((1, 88, half), lambda k: (k, 0, 0))
    y_keep, y_send = pl.pallas_call(
        observe_kernel,
        grid=(batches - 1,),
        in_specs=[
            pl.BlockSpec(flat.shape, lambda k: (0, 0)),
            pl.BlockSpec(background.shape, lambda k: (0, 0)),
            row_spec,
            row_spec,
        ],
        out_specs=(out_spec, out_spec),
        out_shape=(later, later),
        scratch_shapes=observed_scratch,
        compiler_params=params(),
        name="observe",
    )(flat, background, local_cols[1:], local_levs[1:])

    gram_own = plane_sum(keep, send)
    observed = plane_sum(y_keep, y_send)
    by_level = jnp.transpose(perturbations, (1, 0, 2))

    def spread(gram_own):
        own = jnp.concatenate([gram_own] + [swap(gram_own, "owner", hop) for hop in range(1, owners)], axis=0)
        return own, swap(own, "cols", 1)

    product = None
    for index in range(batches - 1):
        own, peer = spread(gram_own)
        operands = [
            all_pairs[index],
            order,
            own,
            peer,
            observed[index],
            tile_half[index + 1].reshape(1, half),
            sigma_half[index + 1, 0].reshape(1, half),
            vals_half[index + 1, 0].reshape(1, half),
        ]
        if index:
            operands.append(product)
        product, gram_own = pl.pallas_call(
            functools.partial(batch_kernel, index == 0),
            out_shape=(jax.ShapeDtypeStruct((tiles // 2, DROWS, 2 * LANES), BF16), gram),
            scratch_shapes=[
                pltpu.VMEM((members * tiles, LANES), F32),
                pltpu.VMEM((tiles, LANES), F32),
                pltpu.VMEM((2 * LANES, half), BF16),
            ],
            compiler_params=params(),
            name="batch",
        )(*operands)

    own, peer = spread(gram_own)
    pairs_of = tiles_dev // 2
    own_product = lax.dynamic_slice_in_dim(product, cols_index * pairs_of, pairs_of, 0)
    mean, out = pl.pallas_call(
        last_kernel,
        out_shape=(
            jax.ShapeDtypeStruct(background.shape, F32),
            jax.ShapeDtypeStruct(by_level.shape, BF16),
        ),
        scratch_shapes=[
            pltpu.VMEM((members * tiles_dev, LANES), F32),
            pltpu.VMEM((tiles_dev, LANES), F32),
            pltpu.VMEM((pairs_of, DROWS, 2 * LANES), BF16),
        ],
        compiler_params=params(),
        name="last",
    )(pairs[batches - 1].astype(F32), order, own, peer, own_product, by_level, background)
    return mean, jnp.transpose(out, (1, 0, 2))


def solution(mesh):
    return jax.shard_map(
        body,
        mesh=mesh,
        in_specs=(
            P(None, "levs", "cols"),
            P("levs", "cols"),
            P(None, "owner"),
            P(None, "owner"),
            P(None, "owner"),
            P(None, "owner"),
            P(None, "cols", None),
        ),
        out_specs=(P("levs", "cols"), P(None, "levs", "cols")),
        check_vma=False,
    )
```

```python
import functools
import math

import jax
import jax.numpy as jnp
from jax import lax
from jax.experimental import pallas as pl
from jax.experimental.pallas import tpu as pltpu
from jax.sharding import PartitionSpec as P

F32 = jnp.float32
BF16 = jnp.bfloat16
LANES = 128
GROUP = 8
CHUNK = 32
PACK = LANES // CHUNK
DROWS = 96
VMEM_BYTES = 40 << 20


def params():
    return pltpu.CompilerParams(vmem_limit_bytes=VMEM_BYTES)


def split2(x):
    high = x.astype(BF16)
    return high, (x - high.astype(F32)).astype(BF16)


def nt_dot(a, b):
    return lax.dot_general(a, b, (((1,), (1,)), ((), ())), preferred_element_type=F32)


def observe_into(y_ref, hot_ref, pert_ref, mean_ref, local_cols, local_levs):
    col_dev, count = hot_ref.shape
    lev_dev = mean_ref.shape[0]
    members = pert_ref.shape[0] // lev_dev
    for start in range(0, col_dev, 256):
        rows = lax.broadcasted_iota(jnp.int32, (256, count), 0) + start
        hot_ref[start : start + 256, :] = jnp.where(rows == local_cols, 1.0, 0.0).astype(BF16)
    lev_hot = lax.broadcasted_iota(jnp.int32, (lev_dev, count), 0) == local_levs
    hot = hot_ref[...]
    step = 16
    for start in range(0, members, step):
        picked = jnp.dot(
            pert_ref[start * lev_dev : (start + step) * lev_dev, :], hot, preferred_element_type=F32
        ).reshape(step, lev_dev, count)
        y_ref[start : start + step, :] = jnp.sum(jnp.where(lev_hot[None], picked, 0.0), axis=1)
    mean = mean_ref[...]
    high = mean.astype(BF16)
    rest = mean - high.astype(F32)
    middle = rest.astype(BF16)
    low = (rest - middle.astype(F32)).astype(BF16)
    picked = jnp.dot(jnp.concatenate([high, middle, low], axis=0), hot, preferred_element_type=F32)
    picked = (
        picked[:lev_dev] + picked[lev_dev : 2 * lev_dev] + picked[2 * lev_dev : 3 * lev_dev]
    )
    total = jnp.sum(jnp.where(lev_hot, picked, 0.0), axis=0, keepdims=True)
    tail = y_ref.shape[0] - members
    first = lax.broadcasted_iota(jnp.int32, (tail, count), 0) == 0
    y_ref[members:, :] = jnp.where(first, jnp.broadcast_to(total, (tail, count)), 0.0)


def block_grams(values, mean_row, sigma, vals, members, store):
    root = math.sqrt(members - 1.0)
    count = values.shape[1]
    scale = 1.0 / (sigma * root)
    innov = (vals - mean_row) / sigma
    wide = values.astype(F32) * (scale * scale)
    pad = LANES - members
    first = lax.broadcasted_iota(jnp.int32, (pad, count), 0) == 0
    last = jnp.where(first, jnp.broadcast_to(scale * innov, (pad, count)), 0.0)
    high, low = split2(jnp.concatenate([wide, last], axis=0))
    for block in range(count // LANES):
        at = slice(block * LANES, (block + 1) * LANES)
        left = jnp.concatenate([values[:, at], values[:, at]], axis=1)
        right = jnp.concatenate([high[:, at], low[:, at]], axis=1)
        store(block, nt_dot(left, right))


def first_kernel(pert_ref, mean_ref, cols_ref, levs_ref, sigma_ref, vals_ref, keep_ref, send_ref, y_ref, hot_ref):
    observe_into(y_ref, hot_ref, pert_ref, mean_ref, cols_ref[...], levs_ref[...])
    members = keep_ref.shape[1]
    own_blocks = keep_ref.shape[0]

    def store(block, product):
        if block < own_blocks:
            keep_ref[block] = product
        else:
            send_ref[block - own_blocks] = product

    block_grams(
        y_ref[:members, :].astype(BF16), y_ref[members : members + 1, :], sigma_ref[...], vals_ref[...], members, store
    )


def observe_kernel(pert_ref, mean_ref, cols_ref, levs_ref, keep_ref, send_ref, y_ref, hot_ref):
    observe_into(y_ref, hot_ref, pert_ref, mean_ref, cols_ref[0], levs_ref[0])
    half = keep_ref.shape[2]
    keep_ref[0] = y_ref[:, :half]
    send_ref[0] = y_ref[:, half:]


def tile_lanes(shape):
    return lax.broadcasted_iota(jnp.int32, shape, 1)


def build_systems(s_ref, pairs, order_ref, own_ref, peer_ref):
    members = own_ref.shape[1]
    spread = nt_dot(order_ref[...], jnp.concatenate([pairs.astype(BF16)] * GROUP, axis=0))
    row = lax.broadcasted_iota(jnp.int32, spread.shape, 0)
    lane = tile_lanes(spread.shape)
    select = jnp.where(row % GROUP == lane // CHUNK, spread, 0.0).astype(BF16)
    rows = s_ref.shape[1]
    out_row = lax.broadcasted_iota(jnp.int32, (rows, LANES), 0)
    out_pack = tile_lanes((rows, LANES)) // CHUNK
    for start in range(0, members, GROUP):
        at = slice(start, start + GROUP)
        stacked = jnp.concatenate(
            [ref[block, at, :] for ref in (own_ref, peer_ref) for block in range(ref.shape[0])], axis=0
        )
        high, low = split2(stacked.T[:rows])
        product = jnp.dot(jnp.concatenate([high, low], axis=1), select, preferred_element_type=F32)
        for part in range(GROUP // PACK):
            first = start + part * PACK
            s_ref[first // PACK] = product[:, part * LANES : (part + 1) * LANES] + jnp.where(
                out_row == first + out_pack, 1.0, 0.0
            )


def invert_factors(s_ref, r_ref, w_ref, members):
    rows = s_ref.shape[1]
    pack = tile_lanes((rows, LANES)) // CHUNK
    within = tile_lanes((rows, LANES)) % CHUNK
    group_row = lax.broadcasted_iota(jnp.int32, (GROUP, LANES), 0)
    count = members // GROUP
    weights = [jnp.zeros((GROUP, LANES), F32) for _ in range(count)]
    picks = [within + p * CHUNK for p in range(PACK)]
    for s in range(count):
        start = s * GROUP
        first = start // PACK
        copies = []
        for a in range(GROUP):
            copies.append(jnp.take_along_axis(s_ref[first + a // PACK], picks[a % PACK], axis=1))
        entry = [[None] * GROUP for _ in range(GROUP)]
        for a in range(GROUP):
            for b in range(a, GROUP):
                entry[a][b] = jnp.broadcast_to(copies[a][start + b : start + b + 1, :], (GROUP, LANES))
        ratio = [[None] * GROUP for _ in range(GROUP)]
        inverse = [None] * GROUP
        for a in range(GROUP):
            inverse[a] = 1.0 / entry[a][a]
            for b in range(a + 1, GROUP):
                ratio[b][a] = entry[a][b] * inverse[a]
            for b in range(a + 1, GROUP):
                for c in range(b, GROUP):
                    entry[b][c] = entry[b][c] - ratio[b][a] * entry[a][c]
        roots = [lax.rsqrt(entry[a][a]) for a in range(GROUP)]
        pieces = rows // GROUP
        lower = [[None] * pieces for _ in range(GROUP)]
        for v in range(pieces):
            for a in range(GROUP):
                if v == s:
                    value = jnp.where(group_row == a, 1.0, 0.0)
                else:
                    value = copies[a][v * GROUP : (v + 1) * GROUP, :]
                for b in range(a):
                    value = value - ratio[a][b] * lower[b][v]
                lower[a][v] = value
        more = start + GROUP < members
        if more:
            for v in range(pieces):
                solved = [None] * GROUP
                for a in range(GROUP - 1, -1, -1):
                    value = lower[a][v] * inverse[a]
                    for b in range(a + 1, GROUP):
                        value = value - ratio[b][a] * solved[b]
                    solved[a] = value
                for a in range(GROUP):
                    value = solved[a]
                    if v == s:
                        value = value + jnp.where(group_row == a, 1.0, 0.0)
                    r_ref[a, v * GROUP : (v + 1) * GROUP, :] = value
        for part in range(GROUP // PACK):

            def merged(v):
                value = lower[part * PACK][v] * roots[part * PACK]
                for p in range(1, PACK):
                    a = part * PACK + p
                    value = jnp.where(pack[:GROUP] == p, lower[a][v] * roots[a], value)
                return value

            halfway = jnp.broadcast_to(merged(count)[0:1, :], (GROUP, LANES))
            for v in range(count):
                if v <= s:
                    value = merged(v)
                    weights[v] = weights[v] + halfway * value
                else:
                    value = jnp.zeros((GROUP, LANES), F32)
                s_ref[first + part, v * GROUP : (v + 1) * GROUP, :] = value
        if more:

            def trailing(index, carry, s=s, start=start, first=first):
                for step in range(GROUP // PACK):
                    block = first + (index + 1) * (GROUP // PACK) + step
                    old = s_ref[block, start : start + GROUP, :]
                    factors = [jnp.broadcast_to(old[a : a + 1, :], (GROUP, LANES)) for a in range(GROUP)]
                    for v in range(pieces):
                        at = slice(v * GROUP, (v + 1) * GROUP)
                        value = s_ref[block, at, :]
                        for a in range(GROUP):
                            value = value - factors[a] * r_ref[a, at, :]
                        s_ref[block, at, :] = value
                return carry

            lax.fori_loop(0, count - 1 - s, trailing, 0)
    for v in range(count):
        total = weights[v]
        shift = CHUNK
        while shift < LANES:
            total = total + pltpu.roll(total, shift, 1)
            shift *= 2
        w_ref[v * GROUP : (v + 1) * GROUP, :] = total


def by_tile(s_ref, w_ref, m_ref, wrow_ref, members):
    one = jnp.where(
        lax.broadcasted_iota(jnp.int32, (LANES, LANES), 0) == tile_lanes((LANES, LANES)), 1.0, 0.0
    ).astype(BF16)
    pad = jnp.zeros((LANES - members, LANES), BF16)
    for block in range(members // PACK):
        value = jnp.concatenate([s_ref[block, :members, :].astype(BF16), pad], axis=0)
        m_ref[block * LANES : (block + 1) * LANES, :] = nt_dot(one, value)
    value = jnp.concatenate([w_ref[...].astype(BF16), pad], axis=0)
    wrow_ref[...] = nt_dot(one[:CHUNK], value)


def factor_chunk(pairs, order_ref, own_ref, peer_ref, s_ref, r_ref, w_ref, m_ref, wrow_ref):
    members = own_ref.shape[1]
    build_systems(s_ref, pairs, order_ref, own_ref, peer_ref)
    invert_factors(s_ref, r_ref, w_ref, members)
    by_tile(s_ref, w_ref, m_ref, wrow_ref, members)


def factor_scratch(members):
    return [
        pltpu.VMEM((members // PACK, members + GROUP, LANES), F32),
        pltpu.VMEM((GROUP, members + GROUP, LANES), F32),
        pltpu.VMEM((members, LANES), F32),
        pltpu.VMEM((members * CHUNK, LANES), F32),
        pltpu.VMEM((CHUNK, LANES), F32),
    ]


def product_of(m_ref, w_ref, tile, old, members):
    rows = m_ref[pl.ds(tile, members, stride=CHUNK), :].astype(BF16)
    tail = DROWS - members
    sub = lax.broadcasted_iota(jnp.int32, (tail, LANES), 0)
    lane = lax.broadcasted_iota(jnp.int32, (tail, LANES), 1)
    weights = jnp.broadcast_to(w_ref[pl.ds(tile, 1), :], (tail, LANES))
    if old is None:
        return jnp.concatenate([rows, jnp.where(sub == 0, weights, 0.0).astype(BF16)], axis=0), None
    ones = (lane >= members) & (lane < members + 2)
    extra = jnp.where(sub == 0, jnp.where(ones, 1.0, weights), 0.0).astype(BF16)
    left = jnp.concatenate([rows, extra], axis=0)[:, :DROWS]
    new = jnp.dot(left, old[0], preferred_element_type=F32)
    if old[1] is not None:
        new = new + jnp.dot(left, old[1], preferred_element_type=F32)
    total = jnp.broadcast_to(new[members : members + 1, :], (tail, LANES))
    high = total.astype(BF16).astype(F32)
    last = jnp.where(sub == 0, high, jnp.where(sub == 1, total - high, 0.0))
    return split2(jnp.concatenate([new[:members], last], axis=0))


def products(m_ref, w_ref, old_ref, new_ref, base, pairs_of, members):
    def pair(index, carry):
        for side in range(2):
            at = slice(side * LANES, (side + 1) * LANES)
            low_at = slice((side + 2) * LANES, (side + 3) * LANES)
            old = None
            if old_ref is not None:
                old = old_ref[base + index, :, at], None
                if old_ref.shape[2] > 2 * LANES:
                    old = old[0], old_ref[base + index, :, low_at]
            high, low = product_of(m_ref, w_ref, index * 2 + side, old, members)
            new_ref[base + index, :, at] = high
            if low is not None:
                new_ref[base + index, :, low_at] = low
        return carry

    lax.fori_loop(0, pairs_of, pair, 0, unroll=2)


def batch_kernel(first, *refs):
    if first:
        (pair_ref, order_ref, own_ref, peer_ref, y_ref, tile_ref, sigma_ref, vals_ref, new_ref, gram_ref, x_ref, *factor) = refs
        old_ref = None
    else:
        (pair_ref, order_ref, own_ref, peer_ref, y_ref, tile_ref, sigma_ref, vals_ref, old_ref, new_ref, gram_ref, x_ref, *factor) = refs
    members = own_ref.shape[1]
    root = math.sqrt(members - 1.0)
    chunks = pair_ref.shape[0] // CHUNK

    def one_chunk(index):
        pairs = pair_ref[pl.ds(index * CHUNK, CHUNK), :]
        factor_chunk(pairs, order_ref, own_ref, peer_ref, *factor)
        products(factor[3], factor[4], old_ref, new_ref, index * (CHUNK // 2), CHUNK // 2, members)

    if chunks == 1:
        one_chunk(0)
    else:
        pl.loop(0, chunks)(one_chunk)
    tile = tile_ref[...]
    count = tile.shape[1]
    start_values = y_ref[:members, :]
    empty = jnp.zeros((LANES - members, count), BF16)
    for side in range(2):
        x_ref[side * LANES : side * LANES + members, :] = jnp.where(tile % 2 == side, start_values, 0.0).astype(BF16)
        x_ref[side * LANES + members : (side + 1) * LANES, :] = empty
    parts = new_ref.shape[2] // (2 * LANES)
    stacked = jnp.concatenate([x_ref[...]] * parts, axis=0)
    half_tile = tile // 2
    per = 4

    def gather(index, total):
        at = new_ref[pl.ds(index * per, per)].reshape(per * DROWS, new_ref.shape[2])
        product = jnp.dot(at, stacked, preferred_element_type=F32)
        for k in range(per):
            total = jnp.where(half_tile == index * per + k, product[k * DROWS : (k + 1) * DROWS], total)
        return total

    now = lax.fori_loop(0, new_ref.shape[0] // per, gather, jnp.zeros((DROWS, count), F32))
    mean_row = y_ref[members : members + 1, :] + (now[members : members + 1] + now[members + 1 : members + 2]) / root

    def store(block, product):
        gram_ref[block] = product

    block_grams(now[:members].astype(BF16), mean_row, sigma_ref[...], vals_ref[...], members, store)


def last_kernel(pair_ref, order_ref, own_ref, peer_ref, old_ref, pert_ref, mean_ref, out_mean_ref, out_ref, new_ref, *factor):
    members = own_ref.shape[1]
    root = math.sqrt(members - 1.0)
    factor_chunk(pair_ref[...], order_ref, own_ref, peer_ref, *factor)
    products(factor[3], factor[4], old_ref, new_ref, 0, new_ref.shape[0], members)
    tiles = new_ref.shape[0] * 2
    width = pert_ref.shape[2] // tiles
    for tile in range(tiles):
        side = tile % 2
        left = new_ref[tile // 2, :, side * LANES : side * LANES + members]
        left_low = new_ref[tile // 2, :, (side + 2) * LANES : (side + 2) * LANES + members]
        at = slice(tile * width, (tile + 1) * width)
        for lev in range(pert_ref.shape[0]):
            pert = pert_ref[lev, :, at]
            new = jnp.dot(left, pert, preferred_element_type=F32) + jnp.dot(
                left_low, pert, preferred_element_type=F32
            )
            out_ref[lev, :, at] = new[:members].astype(BF16)
            gain = new[members : members + 1] + new[members + 1 : members + 2]
            out_mean_ref[lev : lev + 1, at] = mean_ref[lev : lev + 1, at] + gain / root


def swap(x, axis, bit):
    return lax.ppermute(x, axis, [(i, i ^ bit) for i in range(lax.axis_size(axis))])


def upper_bits(axis, first):
    bit, bits = first, []
    while bit < lax.axis_size(axis):
        bits.append(bit)
        bit *= 2
    return bits


def plane_sum(keep, send):
    total = keep + swap(send, "cols", 1)
    for bit in upper_bits("cols", 2):
        total = total + swap(total, "cols", bit)
    for bit in upper_bits("levs", 1):
        total = total + swap(total, "levs", bit)
    return total


def body(perturbations, background, obs_cols, obs_levs, obs_vals, obs_sigma, pairs):
    members, lev_dev, col_dev = perturbations.shape
    batches, obs_own = obs_cols.shape
    tiles_dev, block_count = pairs.shape[1:]
    tile_cols = col_dev // tiles_dev
    cols_size, owners = lax.axis_size("cols"), lax.axis_size("owner")
    tiles = tiles_dev * cols_size
    own_blocks = block_count // owners // 2
    half = obs_own // 2
    cols_index = lax.axis_index("cols")
    core = cols_index % 2
    owner = lax.axis_index("owner")

    def halves(x):
        parts = x.reshape(batches, 2, half)
        return jnp.where(core == 0, parts, parts[:, ::-1])

    cols_half = halves(obs_cols)
    local_cols = (cols_half - cols_index * col_dev).reshape(batches, 1, obs_own)
    local_levs = (halves(obs_levs) - lax.axis_index("levs") * lev_dev).reshape(batches, 1, obs_own)
    sigma_half = halves(obs_sigma)
    vals_half = halves(obs_vals)
    tile_half = cols_half[:, 0] // tile_cols

    all_pairs = pairs.astype(F32)
    for bit in upper_bits("cols", 1):
        other = swap(all_pairs, "cols", bit)
        upper = (cols_index // bit) % 2 == 1
        all_pairs = jnp.where(
            upper, jnp.concatenate([other, all_pairs], axis=1), jnp.concatenate([all_pairs, other], axis=1)
        )

    place = jnp.arange(2 * block_count * GROUP) // GROUP % block_count
    side, rest = place // (block_count // 2), place % (block_count // 2)
    hop, block = rest // own_blocks, rest % own_blocks
    wanted = (owner ^ hop) * (2 * own_blocks) + (core ^ side) * own_blocks + block
    order = (wanted[:, None] == jnp.arange(block_count)[None, :]).astype(BF16)

    flat = perturbations.reshape(members * lev_dev, col_dev)
    gram = jax.ShapeDtypeStruct((own_blocks, members, LANES), F32)
    observed_scratch = [pltpu.VMEM((88, obs_own), F32), pltpu.VMEM((col_dev, obs_own), BF16)]
    keep, send = pl.pallas_call(
        first_kernel,
        out_shape=(gram, gram),
        scratch_shapes=observed_scratch,
        compiler_params=params(),
        name="first",
    )(
        flat,
        background,
        local_cols[0],
        local_levs[0],
        sigma_half[0].reshape(1, obs_own),
        vals_half[0].reshape(1, obs_own),
    )
    later = jax.ShapeDtypeStruct((batches - 1, 88, half), F32)
    row_spec = pl.BlockSpec((1, 1, obs_own), lambda k: (k, 0, 0))
    out_spec = pl.BlockSpec((1, 88, half), lambda k: (k, 0, 0))
    y_keep, y_send = pl.pallas_call(
        observe_kernel,
        grid=(batches - 1,),
        in_specs=[
            pl.BlockSpec(flat.shape, lambda k: (0, 0)),
            pl.BlockSpec(background.shape, lambda k: (0, 0)),
            row_spec,
            row_spec,
        ],
        out_specs=(out_spec, out_spec),
        out_shape=(later, later),
        scratch_shapes=observed_scratch,
        compiler_params=params(),
        name="observe",
    )(flat, background, local_cols[1:], local_levs[1:])

    gram_own = plane_sum(keep, send)
    observed = plane_sum(y_keep, y_send)
    by_level = jnp.transpose(perturbations, (1, 0, 2))

    def spread(gram_own):
        own = jnp.concatenate([gram_own] + [swap(gram_own, "owner", hop) for hop in range(1, owners)], axis=0)
        return own, swap(own, "cols", 1)

    product = None
    for index in range(batches - 1):
        own, peer = spread(gram_own)
        operands = [
            all_pairs[index],
            order,
            own,
            peer,
            observed[index],
            tile_half[index + 1].reshape(1, half),
            sigma_half[index + 1, 0].reshape(1, half),
            vals_half[index + 1, 0].reshape(1, half),
        ]
        if index:
            operands.append(product)
        product, gram_own = pl.pallas_call(
            functools.partial(batch_kernel, index == 0),
            out_shape=(jax.ShapeDtypeStruct((tiles // 2, DROWS, (4 if index else 2) * LANES), BF16), gram),
            scratch_shapes=[
                pltpu.VMEM((2 * LANES, half), BF16),
                *factor_scratch(members),
            ],
            compiler_params=params(),
            name="batch",
        )(*operands)

    own, peer = spread(gram_own)
    pairs_of = tiles_dev // 2
    own_product = lax.dynamic_slice_in_dim(product, cols_index * pairs_of, pairs_of, 0)
    mean, out = pl.pallas_call(
        last_kernel,
        out_shape=(
            jax.ShapeDtypeStruct(background.shape, F32),
            jax.ShapeDtypeStruct(by_level.shape, BF16),
        ),
        scratch_shapes=[
            pltpu.VMEM((pairs_of, DROWS, 4 * LANES), BF16),
            *factor_scratch(members),
        ],
        compiler_params=params(),
        name="last",
    )(
        jnp.pad(pairs[batches - 1].astype(F32), ((0, CHUNK - tiles_dev), (0, 0))),
        order, own, peer, own_product, by_level, background)
    return mean, jnp.transpose(out, (1, 0, 2))


def solution(mesh):
    return jax.shard_map(
        body,
        mesh=mesh,
        in_specs=(
            P(None, "levs", "cols"),
            P("levs", "cols"),
            P(None, "owner"),
            P(None, "owner"),
            P(None, "owner"),
            P(None, "owner"),
            P(None, "cols", None),
        ),
        out_specs=(P("levs", "cols"), P(None, "levs", "cols")),
        check_vma=False,
    )
```

```python
import functools
import math

import jax
import jax.numpy as jnp
from jax import lax
from jax.experimental import pallas as pl
from jax.experimental.pallas import tpu as pltpu
from jax.sharding import PartitionSpec as P

F32 = jnp.float32
BF16 = jnp.bfloat16
LANES = 128
GROUP = 8
CHUNK = 32
DROWS = 96
VMEM_BYTES = 40 << 20
WHOLE_VMEM = 63 << 20


def params(limit=VMEM_BYTES):
    return pltpu.CompilerParams(vmem_limit_bytes=limit)


def split2(x):
    high = x.astype(BF16)
    return high, (x - high.astype(F32)).astype(BF16)


def nt_dot(a, b):
    return lax.dot_general(a, b, (((1,), (1,)), ((), ())), preferred_element_type=F32)


def observe_into(y_ref, hot_ref, pert_ref, mean_ref, local_cols, local_levs, ready=None):
    col_dev, count = hot_ref.shape
    lev_dev = mean_ref.shape[0]
    members = pert_ref.shape[0] // lev_dev
    for start in range(0, col_dev, 256):
        rows = lax.broadcasted_iota(jnp.int32, (256, count), 0) + start
        hot_ref[start : start + 256, :] = jnp.where(rows == local_cols, 1.0, 0.0).astype(BF16)
    lev_hot = lax.broadcasted_iota(jnp.int32, (lev_dev, count), 0) == local_levs
    hot = hot_ref[...]
    step = 16
    for start in range(0, members, step):
        if ready is not None:
            ready(start // step)
        picked = jnp.dot(
            pert_ref[start * lev_dev : (start + step) * lev_dev, :], hot, preferred_element_type=F32
        ).reshape(step, lev_dev, count)
        y_ref[start : start + step, :] = jnp.sum(jnp.where(lev_hot[None], picked, 0.0), axis=1)
    mean = mean_ref[...]
    high = mean.astype(BF16)
    rest = mean - high.astype(F32)
    middle = rest.astype(BF16)
    low = (rest - middle.astype(F32)).astype(BF16)
    picked = jnp.dot(jnp.concatenate([high, middle, low], axis=0), hot, preferred_element_type=F32)
    picked = (
        picked[:lev_dev] + picked[lev_dev : 2 * lev_dev] + picked[2 * lev_dev : 3 * lev_dev]
    )
    total = jnp.sum(jnp.where(lev_hot, picked, 0.0), axis=0, keepdims=True)
    tail = y_ref.shape[0] - members
    first = lax.broadcasted_iota(jnp.int32, (tail, count), 0) == 0
    y_ref[members:, :] = jnp.where(first, jnp.broadcast_to(total, (tail, count)), 0.0)


def half_first(x, core):
    half = x.shape[1] // 2
    return jnp.where(core == 0, x, jnp.concatenate([x[:, half:], x[:, :half]], axis=1))


def packed_grams(values, mean_row, sigma, vals, members):
    root = math.sqrt(members - 1.0)
    count = values.shape[1]
    scale = 1.0 / (sigma * root)
    innov = (vals - mean_row) / sigma
    wide = values.astype(F32) * (scale * scale)
    pad = LANES - members
    first = lax.broadcasted_iota(jnp.int32, (pad, count), 0) == 0
    last = jnp.where(first, jnp.broadcast_to(scale * innov, (pad, count)), 0.0)
    high, low = split2(jnp.concatenate([wide, last], axis=0))
    row = lax.broadcasted_iota(jnp.int32, (members, LANES), 0)
    lane = tile_lanes((members, LANES))
    results = []
    for start in range(0, count, 2 * LANES):
        grams = []
        for at in (slice(start, start + LANES), slice(start + LANES, start + 2 * LANES)):
            left = jnp.concatenate([values[:, at], values[:, at]], axis=1)
            right = jnp.concatenate([high[:, at], low[:, at]], axis=1)
            grams.append(nt_dot(left, right))
        a, b = grams
        diagonal = jnp.sum(jnp.where(lane == row, b, 0.0), axis=1, keepdims=True)
        packed = jnp.where((lane <= row) | (lane == members), a, jnp.where(lane < members, b, 0.0))
        packed = jnp.where(lane == members + 1, b[:, members : members + 1], packed)
        results.append(jnp.where(lane == members + 2, diagonal, packed))
    return results


def unpack_into(full_ref, refs, members):
    row = lax.broadcasted_iota(jnp.int32, (members, LANES), 0)
    lane = tile_lanes((members, LANES))
    index = 0
    for ref in refs:
        for block in range(ref.shape[0]):
            packed = ref[block]
            square = jnp.concatenate([packed, jnp.zeros((LANES - members, LANES), F32)], axis=0)
            turned = square.T[:members]
            full_ref[index] = jnp.where(
                (lane <= row) | (lane == members), packed, jnp.where(lane < members, turned, 0.0)
            )
            other = jnp.where(lane == row, packed[:, members + 2 : members + 3], jnp.where(lane < row, turned, packed))
            full_ref[index + 1] = jnp.where(
                lane < members, other, jnp.where(lane == members, packed[:, members + 1 : members + 2], 0.0)
            )
            index += 2


def observe_batch(y_ref, hot_ref, pert_ref, mean_ref, cols_ref, levs_ref, batch, ready=None):
    core = lax.axis_index("cols") % 2
    col_dev, lev_dev = hot_ref.shape[0], mean_ref.shape[0]
    cols = half_first(cols_ref[batch : batch + 1, :], core) - lax.axis_index("cols") * col_dev
    levs = half_first(levs_ref[batch : batch + 1, :], core) - lax.axis_index("levs") * lev_dev
    observe_into(y_ref, hot_ref, pert_ref, mean_ref, cols, levs, ready)


def store_blocks(y_ref, keep_refs, send_refs):
    for block, ref in enumerate((*keep_refs, *send_refs)):
        ref[...] = y_ref[:, block * LANES : (block + 1) * LANES]


def fetch(sources, held, sems, pert_sems):
    pert_ref, mean_ref = held[:2]
    small = [pltpu.make_async_copy(sources[i], held[i], sems.at[i - 1]) for i in range(1, len(held))]
    step = 16 * mean_ref.shape[0]
    large = [
        pltpu.make_async_copy(sources[0].at[start : start + step, :], pert_ref.at[start : start + step, :], pert_sems.at[i])
        for i, start in enumerate(range(0, pert_ref.shape[0], step))
    ]
    for copy in small + large:
        copy.start()
    for copy in small:
        copy.wait()
    return large


def fetch_scratch(sources, members):
    return [pltpu.VMEM(x.shape, x.dtype) for x in sources] + [
        pltpu.SemaphoreType.DMA((len(sources) - 1,)),
        pltpu.SemaphoreType.DMA((members // 16,)),
    ]


def first_kernel(*refs):
    sources, (keep_ref, send_ref), scratch = refs[:7], refs[7:9], refs[9:]
    held, (sems, pert_sems, y_ref, hot_ref) = scratch[:7], scratch[7:]
    pert_ref, mean_ref, cols_ref, levs_ref, sigma_ref, vals_ref, pair_ref = held
    large = fetch(sources, held, sems, pert_sems)
    core = lax.axis_index("cols") % 2
    members = pert_ref.shape[0] // mean_ref.shape[0]
    batches, tiles_dev, block_count = pair_ref.shape
    observe_batch(y_ref, hot_ref, pert_ref, mean_ref, cols_ref, levs_ref, 0, lambda i: large[i].wait())
    grams = packed_grams(
        y_ref[:members, :].astype(BF16),
        y_ref[members : members + 1, :],
        half_first(sigma_ref[0:1, :], core),
        half_first(vals_ref[0:1, :], core),
        members,
    )
    cols_size = lax.axis_size("cols")
    extra = batches * cols_size
    spread = jnp.where(
        tile_lanes((block_count, LANES)) % block_count == lax.broadcasted_iota(jnp.int32, (block_count, LANES), 0), 1.0, 0.0
    ).astype(BF16)
    mine = tile_lanes((tiles_dev, LANES)) // block_count == lax.broadcasted_iota(jnp.int32, (tiles_dev, LANES), 0)
    row = lax.broadcasted_iota(jnp.int32, (extra, LANES), 0)
    total = jnp.zeros((extra, LANES), F32)
    for batch in range(batches):
        wide = jnp.dot(pair_ref[batch].astype(F32).astype(BF16), spread, preferred_element_type=F32)
        line = jnp.sum(jnp.where(mine, wide, 0.0), axis=0, keepdims=True)
        total = jnp.where(row == batch * cols_size + lax.axis_index("cols"), line, total)
    total = jnp.where(lax.axis_index("levs") == 0, total, 0.0)
    for ref, gram in zip((keep_ref, send_ref), grams):
        ref[:members, :] = gram
        ref[members : members + extra, :] = total
    observe_batch(y_ref, hot_ref, pert_ref, mean_ref, cols_ref, levs_ref, 1)
    rows = y_ref.shape[0]
    places = range(members + extra, keep_ref.shape[0], rows)
    store_blocks(y_ref, *[[ref.at[place : place + rows, :] for place in places] for ref in (keep_ref, send_ref)])


def observe_kernel(batches, pert_ref, mean_ref, cols_ref, levs_ref, keep_ref, send_ref, y_ref, hot_ref):
    per = keep_ref.shape[0] // len(batches)
    for index, batch in enumerate(batches):
        observe_batch(y_ref, hot_ref, pert_ref, mean_ref, cols_ref, levs_ref, batch)
        store_blocks(y_ref, [keep_ref.at[index * per + i] for i in range(per)], [send_ref.at[index * per + i] for i in range(per)])


def tile_lanes(shape):
    return lax.broadcasted_iota(jnp.int32, shape, 1)


def block_order(block_count, own_blocks):
    place = lax.broadcasted_iota(jnp.int32, (2 * block_count * GROUP, LANES), 0) // GROUP % block_count
    side, rest = place // (block_count // 2), place % (block_count // 2)
    hop, block = rest // own_blocks, rest % own_blocks
    core = lax.axis_index("cols") % 2
    wanted = (lax.axis_index("owner") ^ hop) * (2 * own_blocks) + (core ^ side) * own_blocks + block
    return jnp.where(wanted == lax.broadcasted_iota(jnp.int32, wanted.shape, 1) % block_count, 1.0, 0.0).astype(BF16)


def pair_rows(lines, block_count):
    per = LANES // block_count
    rows = jnp.concatenate(
        [jnp.broadcast_to(lines[i : i + 1, :], (per, LANES)) for i in range(lines.shape[0])], axis=0
    )
    row = lax.broadcasted_iota(jnp.int32, rows.shape, 0)
    return jnp.where(tile_lanes(rows.shape) // block_count == row % per, rows, 0.0)


def build_systems(s_ref, pairs, full_ref):
    members = full_ref.shape[1]
    chunk = pairs.shape[0]
    pack = LANES // chunk
    order = block_order(full_ref.shape[0], 2)
    width = GROUP * chunk
    spread = nt_dot(order, jnp.concatenate([pairs.astype(BF16)] * (max(width, LANES) // chunk), axis=0))
    row = lax.broadcasted_iota(jnp.int32, spread.shape, 0)
    lane = tile_lanes(spread.shape)
    sides = max(1, LANES // width)
    select = jnp.concatenate(
        [jnp.where(row % GROUP + side * GROUP == lane // chunk, spread, 0.0) for side in range(sides)], axis=0
    ).astype(BF16)
    rows = s_ref.shape[1]
    out_row = lax.broadcasted_iota(jnp.int32, (rows, LANES), 0)
    out_pack = tile_lanes((rows, LANES)) // chunk
    for start in range(0, members, GROUP * sides):
        parts = []
        for side in range(sides):
            at = slice(start + side * GROUP, start + (side + 1) * GROUP)
            stacked = jnp.concatenate([full_ref[block, at, :] for block in range(full_ref.shape[0])], axis=0)
            parts.extend(split2(stacked.T[:rows]))
        product = jnp.dot(jnp.concatenate(parts, axis=1), select, preferred_element_type=F32)
        for part in range(product.shape[1] // LANES):
            first = start + part * pack
            s_ref[first // pack] = product[:, part * LANES : (part + 1) * LANES] + jnp.where(
                out_row == first + out_pack, 1.0, 0.0
            )


def invert_factors(s_ref, r_ref, m_ref, wrow_ref, members):
    one = jnp.where(
        lax.broadcasted_iota(jnp.int32, (LANES, LANES), 0) == tile_lanes((LANES, LANES)), 1.0, 0.0
    ).astype(BF16)
    pad = jnp.zeros((LANES - members, LANES), F32)
    rows = s_ref.shape[1]
    chunk = wrow_ref.shape[0]
    pack_size = LANES // chunk
    pack = tile_lanes((GROUP, LANES)) // chunk
    within = tile_lanes((rows, LANES)) % chunk
    group_row = lax.broadcasted_iota(jnp.int32, (GROUP, LANES), 0)
    count = members // GROUP
    weights = [jnp.zeros((GROUP, LANES), F32) for _ in range(count)]
    picks = [within + p * chunk for p in range(pack_size)]
    share = min(pack_size, GROUP)
    for s in range(count):
        start = s * GROUP
        first = start // pack_size
        inner = start % pack_size
        copies = []
        for a in range(GROUP):
            copies.append(jnp.take_along_axis(s_ref[first + a // share], picks[inner + a % share], axis=1))
        entry = [[None] * GROUP for _ in range(GROUP)]
        for a in range(GROUP):
            for b in range(a, GROUP):
                entry[a][b] = jnp.broadcast_to(copies[a][start + b : start + b + 1, :], (GROUP, LANES))
        ratio = [[None] * GROUP for _ in range(GROUP)]
        inverse = [None] * GROUP
        for a in range(GROUP):
            inverse[a] = 1.0 / entry[a][a]
            for b in range(a + 1, GROUP):
                ratio[b][a] = entry[a][b] * inverse[a]
            for b in range(a + 1, GROUP):
                for c in range(b, GROUP):
                    entry[b][c] = entry[b][c] - ratio[b][a] * entry[a][c]
        roots = [lax.rsqrt(entry[a][a]) for a in range(GROUP)]
        pieces = rows // GROUP
        lower = [[None] * pieces for _ in range(GROUP)]
        for v in range(pieces):
            for a in range(GROUP):
                if v == s:
                    value = jnp.where(group_row == a, 1.0, 0.0)
                else:
                    value = copies[a][v * GROUP : (v + 1) * GROUP, :]
                for b in range(a):
                    value = value - ratio[a][b] * lower[b][v]
                lower[a][v] = value
        more = start + GROUP < members
        if more:
            for v in range(pieces):
                solved = [None] * GROUP
                for a in range(GROUP - 1, -1, -1):
                    value = lower[a][v] * inverse[a]
                    for b in range(a + 1, GROUP):
                        value = value - ratio[b][a] * solved[b]
                    solved[a] = value
                for a in range(GROUP):
                    value = solved[a]
                    if v == s:
                        value = value + jnp.where(group_row == a, 1.0, 0.0)
                    r_ref[a, v * GROUP : (v + 1) * GROUP, :] = value
        for part in range(GROUP // share):

            def merged(v):
                value = lower[part * share][v] * roots[part * share]
                for p in range(1, share):
                    a = part * share + p
                    value = jnp.where(pack == inner + p, lower[a][v] * roots[a], value)
                return value

            halfway = jnp.broadcast_to(merged(count)[0:1, :], (GROUP, LANES))
            finished = [merged(v) for v in range(s + 1)]
            valid = (pack >= inner) & (pack < inner + share)
            for v in range(s + 1):
                weights[v] = weights[v] + jnp.where(valid, halfway * finished[v], 0.0)
            finished += [jnp.zeros((GROUP, LANES), F32)] * (count - 1 - s)
            block = first + part
            turned = nt_dot(one, jnp.concatenate(finished + [pad], axis=0).astype(BF16))
            at = inner * chunk
            m_ref[block * LANES + at : block * LANES + at + share * chunk, :] = turned[at : at + share * chunk]
        if more:

            def update(block, masked, start=start, inner=inner):
                old = s_ref[block, start : start + GROUP, :]
                if masked:
                    old = jnp.where(pack >= inner + GROUP, old, 0.0)
                factors = [jnp.broadcast_to(old[a : a + 1, :], (GROUP, LANES)) for a in range(GROUP)]
                for v in range(pieces):
                    at = slice(v * GROUP, (v + 1) * GROUP)
                    value = s_ref[block, at, :]
                    for a in range(GROUP):
                        value = value - factors[a] * r_ref[a, at, :]
                    s_ref[block, at, :] = value

            if pack_size > GROUP:
                if inner + GROUP < pack_size:
                    update(first, True)
                for block in range(first + 1, s_ref.shape[0]):
                    update(block, False)
            else:
                per = GROUP // pack_size

                def trailing(index, carry, first=first, update=update, per=per):
                    for step in range(per):
                        update(first + (index + 1) * per + step, False)
                    return carry

                trips = count - 1 - s
                lax.fori_loop(0, trips, trailing, 0, unroll=max(d for d in (1, 2, 3) if trips % d == 0))
    for v in range(count):
        shift = chunk
        while shift < LANES:
            weights[v] = weights[v] + pltpu.roll(weights[v], shift, 1)
            shift *= 2
    wrow_ref[...] = nt_dot(one[:chunk], jnp.concatenate(weights + [pad], axis=0).astype(BF16))


def factor_chunk(pairs, s_ref, r_ref, m_ref, wrow_ref, full_ref):
    build_systems(s_ref, pairs, full_ref)
    invert_factors(s_ref, r_ref, m_ref, wrow_ref, full_ref.shape[1])


def factor_scratch(members, block_count, chunk):
    return [
        pltpu.VMEM((members * chunk // LANES, members + GROUP, LANES), F32),
        pltpu.VMEM((GROUP, members + GROUP, LANES), F32),
        pltpu.VMEM((members * chunk, LANES), F32),
        pltpu.VMEM((chunk, LANES), F32),
        pltpu.VMEM((block_count, members, LANES), F32),
    ]


def product_of(m_ref, w_ref, tile, old, members):
    rows = m_ref[pl.ds(tile, members, stride=w_ref.shape[0]), :].astype(BF16)
    tail = DROWS - members
    sub = lax.broadcasted_iota(jnp.int32, (tail, LANES), 0)
    lane = lax.broadcasted_iota(jnp.int32, (tail, LANES), 1)
    weights = jnp.broadcast_to(w_ref[pl.ds(tile, 1), :], (tail, LANES))
    if old is None:
        return jnp.concatenate([rows, jnp.where(sub == 0, weights, 0.0).astype(BF16)], axis=0), None
    ones = (lane >= members) & (lane < members + 2)
    extra = jnp.where(sub == 0, jnp.where(ones, 1.0, weights), 0.0).astype(BF16)
    left = jnp.concatenate([rows, extra], axis=0)[:, :DROWS]
    new = jnp.dot(left, old[0], preferred_element_type=F32)
    if old[1] is not None:
        new = new + jnp.dot(left, old[1], preferred_element_type=F32)
    total = jnp.broadcast_to(new[members : members + 1, :], (tail, LANES))
    high = total.astype(BF16).astype(F32)
    last = jnp.where(sub == 0, high, jnp.where(sub == 1, total - high, 0.0))
    return split2(jnp.concatenate([new[:members], last], axis=0))


def products(m_ref, w_ref, old_ref, new_ref, base, pairs_of, members, old_base=None):
    old_base = base if old_base is None else old_base

    def pair(index, carry):
        for side in range(2):
            at = slice(side * LANES, (side + 1) * LANES)
            low_at = slice((side + 2) * LANES, (side + 3) * LANES)
            old = None
            if old_ref is not None:
                old = old_ref[old_base + index, :, at], None
                if old_ref.shape[2] > 2 * LANES:
                    old = old[0], old_ref[old_base + index, :, low_at]
            high, low = product_of(m_ref, w_ref, index * 2 + side, old, members)
            new_ref[base + index, :, at] = high
            if low is not None:
                new_ref[base + index, :, low_at] = low
        return carry

    lax.fori_loop(0, pairs_of, pair, 0, unroll=2)


def factor_part(index, total_ref, own_ref, peer_ref, old_ref, new_ref, factor):
    members = own_ref.shape[1]
    block_count = factor[4].shape[0]
    cols_size = lax.axis_size("cols")
    unpack_into(factor[4], (own_ref, peer_ref), members)
    lines = CHUNK * block_count // LANES
    chunks = cols_size // lines

    def one_chunk(chunk):
        rows = total_ref[pl.ds(members + index * cols_size + chunk * lines, lines), :]
        factor_chunk(pair_rows(rows, block_count), *factor)
        products(factor[2], factor[3], old_ref, new_ref, chunk * (CHUNK // 2), CHUNK // 2, members)

    if chunks == 1:
        one_chunk(0)
    else:
        pl.loop(0, chunks)(one_chunk)


def moments_part(index, y, cols_ref, sigma_ref, vals_ref, new_ref, gram_ref, x_ref):
    members = gram_ref.shape[0]
    root = math.sqrt(members - 1.0)
    core = lax.axis_index("cols") % 2
    count = x_ref.shape[1]
    later = slice(index + 1, index + 2)
    tile = half_first(cols_ref[later, :], core)[:, :count] // LANES
    y = jnp.concatenate(y, axis=1)
    start_values = y[:members, :]
    empty = jnp.zeros((LANES - members, count), BF16)
    for side in range(2):
        x_ref[side * LANES : side * LANES + members, :] = jnp.where(tile % 2 == side, start_values, 0.0).astype(BF16)
        x_ref[side * LANES + members : (side + 1) * LANES, :] = empty
    parts = new_ref.shape[2] // (2 * LANES)
    stacked = jnp.concatenate([x_ref[...]] * parts, axis=0)
    half_tile = tile // 2
    per = 4

    def gather(index, total):
        at = new_ref[pl.ds(index * per, per)].reshape(per * DROWS, new_ref.shape[2])
        product = jnp.dot(at, stacked, preferred_element_type=F32)
        for k in range(per):
            total = jnp.where(half_tile == index * per + k, product[k * DROWS : (k + 1) * DROWS], total)
        return total

    now = lax.fori_loop(0, new_ref.shape[0] // per, gather, jnp.zeros((DROWS, count), F32))
    mean_row = y[members : members + 1, :] + (now[members : members + 1] + now[members + 1 : members + 2]) / root
    gram_ref[...] = packed_grams(
        now[:members].astype(BF16),
        mean_row,
        half_first(sigma_ref[later, :], core)[:, :count],
        half_first(vals_ref[later, :], core)[:, :count],
        members,
    )[0]


def batch_kernel(index, total_ref, own_ref, peer_ref, *refs):
    old_ref, y_ref = refs[:2] if index else (None, None)
    cols_ref, sigma_ref, vals_ref, new_ref, gram_ref, x_ref, *factor = refs[2 if index else 0 :]
    members = own_ref.shape[1]
    factor_part(index, total_ref, own_ref, peer_ref, old_ref, new_ref, factor)
    blocks = x_ref.shape[1] // LANES
    if index:
        y = [y_ref[(index - 1) * blocks + block] for block in range(blocks)]
    else:
        rows = members + GROUP
        places = range(total_ref.shape[0] - blocks * rows, total_ref.shape[0], rows)
        y = [total_ref[place : place + rows, :] for place in places]
    moments_part(index, y, cols_ref, sigma_ref, vals_ref, new_ref, gram_ref, x_ref)


def last_kernel(batches, total_ref, own_ref, peer_ref, old_ref, pert_ref, mean_ref, out_mean_ref, out_ref, new_ref, *factor):
    members = own_ref.shape[1]
    root = math.sqrt(members - 1.0)
    tiles = new_ref.shape[0] * 2
    unpack_into(factor[4], (own_ref, peer_ref), members)
    cols_size = lax.axis_size("cols")
    line = total_ref[pl.ds(members + (batches - 1) * cols_size + lax.axis_index("cols"), 1), :]
    pairs = pair_rows(line, factor[4].shape[0])
    factor_chunk(pairs, *factor)
    own_first = lax.axis_index("cols") * new_ref.shape[0]
    products(factor[2], factor[3], old_ref, new_ref, 0, new_ref.shape[0], members, own_first)
    width = pert_ref.shape[2] // tiles
    levs = pert_ref.shape[0]
    step = 16
    turn_shape = (step * levs, step * levs)
    turn_row = lax.broadcasted_iota(jnp.int32, turn_shape, 0)
    source = turn_row % levs * step + turn_row // levs
    turn = jnp.where(lax.broadcasted_iota(jnp.int32, turn_shape, 1) == source, 1.0, 0.0).astype(BF16)
    for pair in range(tiles // 2):
        news = [[] for _ in range(levs)]
        for side in range(2):
            left = new_ref[pair, :, side * LANES : side * LANES + members]
            left_low = new_ref[pair, :, (side + 2) * LANES : (side + 2) * LANES + members]
            at = slice((pair * 2 + side) * width, (pair * 2 + side + 1) * width)
            for lev in range(levs):
                pert = pert_ref[lev, :, at]
                new = jnp.dot(left, pert, preferred_element_type=F32) + jnp.dot(
                    left_low, pert, preferred_element_type=F32
                )
                gain = new[members : members + 1] + new[members + 1 : members + 2]
                out_mean_ref[lev : lev + 1, at] = mean_ref[lev : lev + 1, at] + gain / root
                news[lev].append(new[:members].astype(BF16))
        news = [jnp.concatenate(sides, axis=1) for sides in news]
        at = slice(pair * 2 * width, (pair + 1) * 2 * width)
        for start in range(0, members, step):
            block = jnp.concatenate([new[start : start + step] for new in news], axis=0)
            turned = jnp.dot(turn, block, preferred_element_type=F32).astype(BF16)
            out_ref[start * levs : (start + step) * levs, at] = turned


def swap(x, axis, bit):
    return lax.ppermute(x, axis, [(i, i ^ bit) for i in range(lax.axis_size(axis))])


def upper_bits(axis, first):
    bit, bits = first, []
    while bit < lax.axis_size(axis):
        bits.append(bit)
        bit *= 2
    return bits


def after(x, *others):
    return lax.optimization_barrier((x, *others))[0]


def body(perturbations, background, obs_cols, obs_levs, obs_vals, obs_sigma, pairs):
    members, lev_dev, col_dev = perturbations.shape
    batches, obs_own = obs_cols.shape
    tiles_dev, block_count = pairs.shape[1:]
    cols_size, owners = lax.axis_size("cols"), lax.axis_size("owner")
    tiles = tiles_dev * cols_size
    half = obs_own // 2
    blocks = half // LANES
    assert block_count // owners // 2 == blocks == 2
    assert col_dev == tiles_dev * LANES == LANES * LANES // block_count

    flat = perturbations.reshape(members * lev_dev, col_dev)
    rows = members + GROUP
    observed_scratch = [pltpu.VMEM((rows, obs_own), F32), pltpu.VMEM((col_dev, obs_own), BF16)]
    message = jax.ShapeDtypeStruct((members + batches * cols_size + blocks * rows, LANES), F32)
    sources = (flat, background, obs_cols, obs_levs, obs_sigma, obs_vals, pairs)
    keep, send = pl.pallas_call(
        first_kernel,
        in_specs=[pl.BlockSpec(memory_space=pltpu.MemorySpace.HBM)] * len(sources),
        out_shape=(message, message),
        scratch_shapes=fetch_scratch(sources, members) + observed_scratch,
        compiler_params=params(WHOLE_VMEM),
        name="first",
    )(*sources)

    def observe(which, obs_cols):
        shape = jax.ShapeDtypeStruct((blocks * len(which), rows, LANES), F32)
        return pl.pallas_call(
            functools.partial(observe_kernel, which),
            out_shape=(shape, shape),
            scratch_shapes=observed_scratch,
            compiler_params=params(),
            cost_estimate=pl.CostEstimate(flops=2 * 10**9 * len(which), bytes_accessed=10**7, transcendentals=0),
            name="observe",
        )(flat, background, obs_cols, obs_levs)

    stages = [("cols", bit) for bit in upper_bits("cols", 2)] + [("levs", bit) for bit in upper_bits("levs", 1)]
    total = keep + swap(send, "cols", 1)
    for axis, bit in stages:
        total = total + swap(total, axis, bit)
    gram_own = total[:members]

    def spread(gram_own):
        own = jnp.stack([gram_own] + [swap(gram_own, "owner", hop) for hop in range(1, owners)])
        return own, swap(own, "cols", 1)

    product = None
    for index in range(batches - 1):
        if index == 0:
            y_keep, y_send = observe(tuple(range(2, batches)), after(obs_cols, gram_own))
        own, peer = spread(gram_own)
        if index == 0:
            own = after(own, y_keep)
            y_later = y_keep + swap(y_send, "cols", 1)
            for axis, bit in stages:
                y_later = y_later + swap(y_later, axis, bit)
        if index == 1:
            by_level = jnp.transpose(after(perturbations, gram_own), (1, 0, 2))
            own = after(own, by_level)
        product, gram_own = pl.pallas_call(
            functools.partial(batch_kernel, index),
            out_shape=(
                jax.ShapeDtypeStruct((tiles // 2, DROWS, (4 if index else 2) * LANES), BF16),
                jax.ShapeDtypeStruct((members, LANES), F32),
            ),
            scratch_shapes=[pltpu.VMEM((2 * LANES, half), BF16), *factor_scratch(members, block_count, CHUNK)],
            compiler_params=params(),
            cost_estimate=pl.CostEstimate(flops=10**10, bytes_accessed=10**7, transcendentals=0),
            name="batch",
        )(total, own, peer, *((product, y_later) if index else ()), obs_cols, obs_sigma, obs_vals)

    own, peer = spread(gram_own)
    pairs_of = tiles_dev // 2
    mean, out = pl.pallas_call(
        functools.partial(last_kernel, batches),
        out_shape=(
            jax.ShapeDtypeStruct(background.shape, F32),
            jax.ShapeDtypeStruct(flat.shape, BF16),
        ),
        scratch_shapes=[
            pltpu.VMEM((pairs_of, DROWS, 4 * LANES), BF16),
            *factor_scratch(members, block_count, tiles_dev),
        ],
        compiler_params=params(),
        name="last",
    )(total, own, peer, product, by_level, background)
    return mean, out.reshape(perturbations.shape)


def solution(mesh):
    return jax.shard_map(
        body,
        mesh=mesh,
        in_specs=(
            P(None, "levs", "cols"),
            P("levs", "cols"),
            P(None, "owner"),
            P(None, "owner"),
            P(None, "owner"),
            P(None, "owner"),
            P(None, "cols", None),
        ),
        out_specs=(P("levs", "cols"), P(None, "levs", "cols")),
        check_vma=False,
    )
```

```python
import functools
import math

import jax
import jax.numpy as jnp
from jax import lax
from jax.experimental import pallas as pl
from jax.experimental.pallas import tpu as pltpu
from jax.sharding import PartitionSpec as P

F32 = jnp.float32
BF16 = jnp.bfloat16
LANES = 128
GROUP = 8
CHUNK = 32
DROWS = 96
VMEM_BYTES = 40 << 20
WHOLE_VMEM = 63 << 20


def params(limit=VMEM_BYTES):
    return pltpu.CompilerParams(vmem_limit_bytes=limit)


def split2(x):
    high = x.astype(BF16)
    return high, (x - high.astype(F32)).astype(BF16)


def nt_dot(a, b):
    return lax.dot_general(a, b, (((1,), (1,)), ((), ())), preferred_element_type=F32)


def observe_into(y_ref, hot_ref, pert_ref, mean_ref, local_cols, local_levs, ready=None):
    col_dev, count = hot_ref.shape
    lev_dev = mean_ref.shape[0]
    members = pert_ref.shape[0] // lev_dev
    for start in range(0, col_dev, 256):
        rows = lax.broadcasted_iota(jnp.int32, (256, count), 0) + start
        hot_ref[start : start + 256, :] = jnp.where(rows == local_cols, 1.0, 0.0).astype(BF16)
    lev_hot = lax.broadcasted_iota(jnp.int32, (lev_dev, count), 0) == local_levs
    hot = hot_ref[...]
    step = 16
    for start in range(0, members, step):
        if ready is not None:
            ready(start // step)
        picked = jnp.dot(
            pert_ref[start * lev_dev : (start + step) * lev_dev, :], hot, preferred_element_type=F32
        ).reshape(step, lev_dev, count)
        y_ref[start : start + step, :] = jnp.sum(jnp.where(lev_hot[None], picked, 0.0), axis=1)
    mean = mean_ref[...]
    high = mean.astype(BF16)
    rest = mean - high.astype(F32)
    middle = rest.astype(BF16)
    low = (rest - middle.astype(F32)).astype(BF16)
    picked = jnp.dot(jnp.concatenate([high, middle, low], axis=0), hot, preferred_element_type=F32)
    picked = (
        picked[:lev_dev] + picked[lev_dev : 2 * lev_dev] + picked[2 * lev_dev : 3 * lev_dev]
    )
    total = jnp.sum(jnp.where(lev_hot, picked, 0.0), axis=0, keepdims=True)
    tail = y_ref.shape[0] - members
    first = lax.broadcasted_iota(jnp.int32, (tail, count), 0) == 0
    y_ref[members:, :] = jnp.where(first, jnp.broadcast_to(total, (tail, count)), 0.0)


def half_first(x, core):
    half = x.shape[1] // 2
    return jnp.where(core == 0, x, jnp.concatenate([x[:, half:], x[:, :half]], axis=1))


def packed_grams(values, mean_row, sigma, vals, members):
    root = math.sqrt(members - 1.0)
    count = values.shape[1]
    scale = 1.0 / (sigma * root)
    innov = (vals - mean_row) / sigma
    wide = values.astype(F32) * (scale * scale)
    pad = LANES - members
    first = lax.broadcasted_iota(jnp.int32, (pad, count), 0) == 0
    last = jnp.where(first, jnp.broadcast_to(scale * innov, (pad, count)), 0.0)
    high, low = split2(jnp.concatenate([wide, last], axis=0))
    row = lax.broadcasted_iota(jnp.int32, (members, LANES), 0)
    lane = tile_lanes((members, LANES))
    results = []
    for start in range(0, count, 2 * LANES):
        grams = []
        for at in (slice(start, start + LANES), slice(start + LANES, start + 2 * LANES)):
            left = jnp.concatenate([values[:, at], values[:, at]], axis=1)
            right = jnp.concatenate([high[:, at], low[:, at]], axis=1)
            grams.append(nt_dot(left, right))
        a, b = grams
        diagonal = jnp.sum(jnp.where(lane == row, b, 0.0), axis=1, keepdims=True)
        packed = jnp.where((lane <= row) | (lane == members), a, jnp.where(lane < members, b, 0.0))
        packed = jnp.where(lane == members + 1, b[:, members : members + 1], packed)
        results.append(jnp.where(lane == members + 2, diagonal, packed))
    return results


def unpack_into(full_ref, refs, members):
    row = lax.broadcasted_iota(jnp.int32, (members, LANES), 0)
    lane = tile_lanes((members, LANES))
    index = 0
    for ref in refs:
        for block in range(ref.shape[0]):
            packed = ref[block]
            square = jnp.concatenate([packed, jnp.zeros((LANES - members, LANES), F32)], axis=0)
            turned = square.T[:members]
            full_ref[index] = jnp.where(
                (lane <= row) | (lane == members), packed, jnp.where(lane < members, turned, 0.0)
            )
            other = jnp.where(lane == row, packed[:, members + 2 : members + 3], jnp.where(lane < row, turned, packed))
            full_ref[index + 1] = jnp.where(
                lane < members, other, jnp.where(lane == members, packed[:, members + 1 : members + 2], 0.0)
            )
            index += 2


def observe_batch(y_ref, hot_ref, pert_ref, mean_ref, cols_ref, levs_ref, batch, ready=None):
    core = lax.axis_index("cols") % 2
    col_dev, lev_dev = hot_ref.shape[0], mean_ref.shape[0]
    cols = half_first(cols_ref[batch : batch + 1, :], core) - lax.axis_index("cols") * col_dev
    levs = half_first(levs_ref[batch : batch + 1, :], core) - lax.axis_index("levs") * lev_dev
    observe_into(y_ref, hot_ref, pert_ref, mean_ref, cols, levs, ready)


def store_blocks(y_ref, keep_refs, send_refs):
    for block, ref in enumerate((*keep_refs, *send_refs)):
        ref[...] = y_ref[:, block * LANES : (block + 1) * LANES]


def fetch(sources, held, sems, pert_sems):
    pert_ref, mean_ref = held[:2]
    small = [pltpu.make_async_copy(sources[i], held[i], sems.at[i - 1]) for i in range(1, len(held))]
    step = 16 * mean_ref.shape[0]
    large = [
        pltpu.make_async_copy(sources[0].at[start : start + step, :], pert_ref.at[start : start + step, :], pert_sems.at[i])
        for i, start in enumerate(range(0, pert_ref.shape[0], step))
    ]
    for copy in small + large:
        copy.start()
    for copy in small:
        copy.wait()
    return large


def fetch_scratch(sources, members):
    return [pltpu.VMEM(x.shape, x.dtype) for x in sources] + [
        pltpu.SemaphoreType.DMA((len(sources) - 1,)),
        pltpu.SemaphoreType.DMA((members // 16,)),
    ]


def first_kernel(*refs):
    sources, (keep_ref, send_ref), scratch = refs[:7], refs[7:9], refs[9:]
    held, (sems, pert_sems, y_ref, hot_ref) = scratch[:7], scratch[7:]
    pert_ref, mean_ref, cols_ref, levs_ref, sigma_ref, vals_ref, pair_ref = held
    large = fetch(sources, held, sems, pert_sems)
    core = lax.axis_index("cols") % 2
    members = pert_ref.shape[0] // mean_ref.shape[0]
    batches, tiles_dev, block_count = pair_ref.shape
    observe_batch(y_ref, hot_ref, pert_ref, mean_ref, cols_ref, levs_ref, 0, lambda i: large[i].wait())
    grams = packed_grams(
        y_ref[:members, :].astype(BF16),
        y_ref[members : members + 1, :],
        half_first(sigma_ref[0:1, :], core),
        half_first(vals_ref[0:1, :], core),
        members,
    )
    cols_size = lax.axis_size("cols")
    extra = batches * cols_size
    spread = jnp.where(
        tile_lanes((block_count, LANES)) % block_count == lax.broadcasted_iota(jnp.int32, (block_count, LANES), 0), 1.0, 0.0
    ).astype(BF16)
    mine = tile_lanes((tiles_dev, LANES)) // block_count == lax.broadcasted_iota(jnp.int32, (tiles_dev, LANES), 0)
    row = lax.broadcasted_iota(jnp.int32, (extra, LANES), 0)
    total = jnp.zeros((extra, LANES), F32)
    for batch in range(batches):
        wide = jnp.dot(pair_ref[batch].astype(F32).astype(BF16), spread, preferred_element_type=F32)
        line = jnp.sum(jnp.where(mine, wide, 0.0), axis=0, keepdims=True)
        total = jnp.where(row == batch * cols_size + lax.axis_index("cols"), line, total)
    total = jnp.where(lax.axis_index("levs") == 0, total, 0.0)
    for ref, gram in zip((keep_ref, send_ref), grams):
        ref[:members, :] = gram
        ref[members : members + extra, :] = total
    observe_batch(y_ref, hot_ref, pert_ref, mean_ref, cols_ref, levs_ref, 1)
    rows = y_ref.shape[0]
    places = range(members + extra, keep_ref.shape[0], rows)
    store_blocks(y_ref, *[[ref.at[place : place + rows, :] for place in places] for ref in (keep_ref, send_ref)])


def observe_kernel(batches, pert_ref, mean_ref, cols_ref, levs_ref, keep_ref, send_ref, y_ref, hot_ref):
    per = keep_ref.shape[0] // len(batches)
    for index, batch in enumerate(batches):
        observe_batch(y_ref, hot_ref, pert_ref, mean_ref, cols_ref, levs_ref, batch)
        store_blocks(y_ref, [keep_ref.at[index * per + i] for i in range(per)], [send_ref.at[index * per + i] for i in range(per)])


def tile_lanes(shape):
    return lax.broadcasted_iota(jnp.int32, shape, 1)


def block_order(block_count, own_blocks):
    place = lax.broadcasted_iota(jnp.int32, (2 * block_count * GROUP, LANES), 0) // GROUP % block_count
    side, rest = place // (block_count // 2), place % (block_count // 2)
    hop, block = rest // own_blocks, rest % own_blocks
    core = lax.axis_index("cols") % 2
    wanted = (lax.axis_index("owner") ^ hop) * (2 * own_blocks) + (core ^ side) * own_blocks + block
    return jnp.where(wanted == lax.broadcasted_iota(jnp.int32, wanted.shape, 1) % block_count, 1.0, 0.0).astype(BF16)


def pair_rows(lines, block_count):
    per = LANES // block_count
    rows = jnp.concatenate(
        [jnp.broadcast_to(lines[i : i + 1, :], (per, LANES)) for i in range(lines.shape[0])], axis=0
    )
    row = lax.broadcasted_iota(jnp.int32, rows.shape, 0)
    return jnp.where(tile_lanes(rows.shape) // block_count == row % per, rows, 0.0)


def build_systems(s_ref, pairs, full_ref):
    members = full_ref.shape[1]
    chunk = pairs.shape[0]
    pack = LANES // chunk
    order = block_order(full_ref.shape[0], 2)
    width = GROUP * chunk
    spread = nt_dot(order, jnp.concatenate([pairs.astype(BF16)] * (max(width, LANES) // chunk), axis=0))
    row = lax.broadcasted_iota(jnp.int32, spread.shape, 0)
    lane = tile_lanes(spread.shape)
    sides = max(1, LANES // width)
    select = jnp.concatenate(
        [jnp.where(row % GROUP + side * GROUP == lane // chunk, spread, 0.0) for side in range(sides)], axis=0
    ).astype(BF16)
    rows = s_ref.shape[1]
    out_row = lax.broadcasted_iota(jnp.int32, (rows, LANES), 0)
    out_pack = tile_lanes((rows, LANES)) // chunk
    for start in range(0, members, GROUP * sides):
        parts = []
        for side in range(sides):
            at = slice(start + side * GROUP, start + (side + 1) * GROUP)
            stacked = jnp.concatenate([full_ref[block, at, :] for block in range(full_ref.shape[0])], axis=0)
            parts.extend(split2(stacked.T[:rows]))
        product = jnp.dot(jnp.concatenate(parts, axis=1), select, preferred_element_type=F32)
        for part in range(product.shape[1] // LANES):
            first = start + part * pack
            s_ref[first // pack] = product[:, part * LANES : (part + 1) * LANES] + jnp.where(
                out_row == first + out_pack, 1.0, 0.0
            )


def invert_factors(s_ref, r_ref, m_ref, wrow_ref, members):
    one = jnp.where(
        lax.broadcasted_iota(jnp.int32, (LANES, LANES), 0) == tile_lanes((LANES, LANES)), 1.0, 0.0
    ).astype(BF16)
    pad = jnp.zeros((LANES - members, LANES), F32)
    rows = s_ref.shape[1]
    chunk = wrow_ref.shape[0]
    pack_size = LANES // chunk
    pack = tile_lanes((GROUP, LANES)) // chunk
    within = tile_lanes((rows, LANES)) % chunk
    group_row = lax.broadcasted_iota(jnp.int32, (GROUP, LANES), 0)
    count = members // GROUP
    weights = [jnp.zeros((GROUP, LANES), F32) for _ in range(count)]
    picks = [within + p * chunk for p in range(pack_size)]
    share = min(pack_size, GROUP)
    for s in range(count):
        start = s * GROUP
        first = start // pack_size
        inner = start % pack_size
        copies = []
        for a in range(GROUP):
            copies.append(jnp.take_along_axis(s_ref[first + a // share], picks[inner + a % share], axis=1))
        entry = [[None] * GROUP for _ in range(GROUP)]
        for a in range(GROUP):
            for b in range(a, GROUP):
                entry[a][b] = jnp.broadcast_to(copies[a][start + b : start + b + 1, :], (GROUP, LANES))
        ratio = [[None] * GROUP for _ in range(GROUP)]
        inverse = [None] * GROUP
        for a in range(GROUP):
            inverse[a] = pl.reciprocal(entry[a][a])
            for b in range(a + 1, GROUP):
                ratio[b][a] = entry[a][b] * inverse[a]
            for b in range(a + 1, GROUP):
                for c in range(b, GROUP):
                    entry[b][c] = entry[b][c] - ratio[b][a] * entry[a][c]
        roots = [lax.rsqrt(entry[a][a]) for a in range(GROUP)]
        pieces = rows // GROUP
        lower = [[None] * pieces for _ in range(GROUP)]
        for v in range(pieces):
            for a in range(GROUP):
                if v == s:
                    value = jnp.where(group_row == a, 1.0, 0.0)
                else:
                    value = copies[a][v * GROUP : (v + 1) * GROUP, :]
                for b in range(a):
                    value = value - ratio[a][b] * lower[b][v]
                lower[a][v] = value
        more = start + GROUP < members
        if more:
            for v in range(pieces):
                solved = [None] * GROUP
                for a in range(GROUP - 1, -1, -1):
                    value = lower[a][v] * inverse[a]
                    for b in range(a + 1, GROUP):
                        value = value - ratio[b][a] * solved[b]
                    solved[a] = value
                for a in range(GROUP):
                    value = solved[a]
                    if v == s:
                        value = value + jnp.where(group_row == a, 1.0, 0.0)
                    r_ref[s % 2 * GROUP + a, v * GROUP : (v + 1) * GROUP, :] = value
        for part in range(GROUP // share):

            def merged(v):
                value = lower[part * share][v] * roots[part * share]
                for p in range(1, share):
                    a = part * share + p
                    value = jnp.where(pack == inner + p, lower[a][v] * roots[a], value)
                return value

            halfway = jnp.broadcast_to(merged(count)[0:1, :], (GROUP, LANES))
            finished = [merged(v) for v in range(s + 1)]
            valid = (pack >= inner) & (pack < inner + share)
            for v in range(s + 1):
                weights[v] = weights[v] + jnp.where(valid, halfway * finished[v], 0.0)
            finished += [jnp.zeros((GROUP, LANES), F32)] * (count - 1 - s)
            block = first + part
            turned = nt_dot(one, jnp.concatenate(finished + [pad], axis=0).astype(BF16))
            at = inner * chunk
            m_ref[block * LANES + at : block * LANES + at + share * chunk, :] = turned[at : at + share * chunk]
        if more:

            def update(block, masked, start=start, inner=inner, side=s % 2 * GROUP):
                old = s_ref[block, start : start + GROUP, :]
                if masked:
                    old = jnp.where(pack >= inner + GROUP, old, 0.0)
                factors = [jnp.broadcast_to(old[a : a + 1, :], (GROUP, LANES)) for a in range(GROUP)]
                for v in range(pieces):
                    at = slice(v * GROUP, (v + 1) * GROUP)
                    value = s_ref[block, at, :]
                    for a in range(GROUP):
                        value = value - factors[a] * r_ref[side + a, at, :]
                    s_ref[block, at, :] = value

            if pack_size > GROUP:
                if inner + GROUP < pack_size:
                    update(first, True)
                for block in range(first + 1, s_ref.shape[0]):
                    update(block, False)
            else:
                per = GROUP // pack_size

                def trailing(index, carry, first=first, update=update, per=per):
                    for step in range(per):
                        update(first + (index + 1) * per + step, False)
                    return carry

                trips = count - 1 - s
                lax.fori_loop(0, trips, trailing, 0, unroll=True)
    for v in range(count):
        shift = chunk
        while shift < LANES:
            weights[v] = weights[v] + pltpu.roll(weights[v], shift, 1)
            shift *= 2
    wrow_ref[...] = nt_dot(one[:chunk], jnp.concatenate(weights + [pad], axis=0).astype(BF16))


def factor_chunk(pairs, s_ref, r_ref, m_ref, wrow_ref, full_ref):
    build_systems(s_ref, pairs, full_ref)
    invert_factors(s_ref, r_ref, m_ref, wrow_ref, full_ref.shape[1])


def factor_scratch(members, block_count, chunk):
    return [
        pltpu.VMEM((members * chunk // LANES, members + GROUP, LANES), F32),
        pltpu.VMEM((2 * GROUP, members + GROUP, LANES), F32),
        pltpu.VMEM((members * chunk, LANES), F32),
        pltpu.VMEM((chunk, LANES), F32),
        pltpu.VMEM((block_count, members, LANES), F32),
    ]


def product_of(m_ref, w_ref, tile, old, members):
    rows = m_ref[pl.ds(tile, members, stride=w_ref.shape[0]), :].astype(BF16)
    tail = DROWS - members
    sub = lax.broadcasted_iota(jnp.int32, (tail, LANES), 0)
    lane = lax.broadcasted_iota(jnp.int32, (tail, LANES), 1)
    weights = jnp.broadcast_to(w_ref[pl.ds(tile, 1), :], (tail, LANES))
    if old is None:
        return jnp.concatenate([rows, jnp.where(sub == 0, weights, 0.0).astype(BF16)], axis=0), None
    ones = (lane >= members) & (lane < members + 2)
    extra = jnp.where(sub == 0, jnp.where(ones, 1.0, weights), 0.0).astype(BF16)
    left = jnp.concatenate([rows, extra], axis=0)[:, :DROWS]
    new = jnp.dot(left, old[0], preferred_element_type=F32)
    if old[1] is not None:
        new = new + jnp.dot(left, old[1], preferred_element_type=F32)
    total = jnp.broadcast_to(new[members : members + 1, :], (tail, LANES))
    high = total.astype(BF16).astype(F32)
    last = jnp.where(sub == 0, high, jnp.where(sub == 1, total - high, 0.0))
    return split2(jnp.concatenate([new[:members], last], axis=0))


def products(m_ref, w_ref, old_ref, new_ref, base, pairs_of, members, old_base=None):
    old_base = base if old_base is None else old_base

    def pair(index, carry):
        for side in range(2):
            at = slice(side * LANES, (side + 1) * LANES)
            low_at = slice((side + 2) * LANES, (side + 3) * LANES)
            old = None
            if old_ref is not None:
                old = old_ref[old_base + index, :, at], None
                if old_ref.shape[2] > 2 * LANES:
                    old = old[0], old_ref[old_base + index, :, low_at]
            high, low = product_of(m_ref, w_ref, index * 2 + side, old, members)
            new_ref[base + index, :, at] = high
            if low is not None:
                new_ref[base + index, :, low_at] = low
        return carry

    lax.fori_loop(0, pairs_of, pair, 0, unroll=4)


def factor_part(index, total_ref, own_ref, peer_ref, old_ref, new_ref, factor):
    members = own_ref.shape[1]
    block_count = factor[4].shape[0]
    cols_size = lax.axis_size("cols")
    unpack_into(factor[4], (own_ref, peer_ref), members)
    lines = CHUNK * block_count // LANES
    chunks = cols_size // lines

    def one_chunk(chunk):
        rows = total_ref[pl.ds(members + index * cols_size + chunk * lines, lines), :]
        factor_chunk(pair_rows(rows, block_count), *factor)
        products(factor[2], factor[3], old_ref, new_ref, chunk * (CHUNK // 2), CHUNK // 2, members)

    if chunks == 1:
        one_chunk(0)
    else:
        pl.loop(0, chunks)(one_chunk)


def moments_part(index, y, cols_ref, sigma_ref, vals_ref, new_ref, gram_ref, x_ref):
    members = gram_ref.shape[0]
    root = math.sqrt(members - 1.0)
    core = lax.axis_index("cols") % 2
    count = x_ref.shape[1]
    later = slice(index + 1, index + 2)
    tile = half_first(cols_ref[later, :], core)[:, :count] // LANES
    y = jnp.concatenate(y, axis=1)
    start_values = y[:members, :]
    empty = jnp.zeros((LANES - members, count), BF16)
    for side in range(2):
        x_ref[side * LANES : side * LANES + members, :] = jnp.where(tile % 2 == side, start_values, 0.0).astype(BF16)
        x_ref[side * LANES + members : (side + 1) * LANES, :] = empty
    parts = new_ref.shape[2] // (2 * LANES)
    stacked = jnp.concatenate([x_ref[...]] * parts, axis=0)
    half_tile = tile // 2
    per = 4

    def gather(index, total):
        at = new_ref[pl.ds(index * per, per)].reshape(per * DROWS, new_ref.shape[2])
        product = jnp.dot(at, stacked, preferred_element_type=F32)
        for k in range(per):
            total = jnp.where(half_tile == index * per + k, product[k * DROWS : (k + 1) * DROWS], total)
        return total

    now = lax.fori_loop(0, new_ref.shape[0] // per, gather, jnp.zeros((DROWS, count), F32), unroll=4)
    mean_row = y[members : members + 1, :] + (now[members : members + 1] + now[members + 1 : members + 2]) / root
    gram_ref[...] = packed_grams(
        now[:members].astype(BF16),
        mean_row,
        half_first(sigma_ref[later, :], core)[:, :count],
        half_first(vals_ref[later, :], core)[:, :count],
        members,
    )[0]


def batch_kernel(index, total_ref, own_ref, peer_ref, *refs):
    old_ref, y_ref = refs[:2] if index else (None, None)
    cols_ref, sigma_ref, vals_ref, new_ref, gram_ref, x_ref, *factor = refs[2 if index else 0 :]
    members = own_ref.shape[1]
    factor_part(index, total_ref, own_ref, peer_ref, old_ref, new_ref, factor)
    blocks = x_ref.shape[1] // LANES
    if index:
        y = [y_ref[(index - 1) * blocks + block] for block in range(blocks)]
    else:
        rows = members + GROUP
        places = range(total_ref.shape[0] - blocks * rows, total_ref.shape[0], rows)
        y = [total_ref[place : place + rows, :] for place in places]
    moments_part(index, y, cols_ref, sigma_ref, vals_ref, new_ref, gram_ref, x_ref)


def last_kernel(batches, total_ref, own_ref, peer_ref, old_ref, pert_ref, mean_ref, out_mean_ref, out_ref, new_ref, *factor):
    members = own_ref.shape[1]
    root = math.sqrt(members - 1.0)
    tiles = new_ref.shape[0] * 2
    unpack_into(factor[4], (own_ref, peer_ref), members)
    cols_size = lax.axis_size("cols")
    line = total_ref[pl.ds(members + (batches - 1) * cols_size + lax.axis_index("cols"), 1), :]
    pairs = pair_rows(line, factor[4].shape[0])
    factor_chunk(pairs, *factor)
    own_first = lax.axis_index("cols") * new_ref.shape[0]
    products(factor[2], factor[3], old_ref, new_ref, 0, new_ref.shape[0], members, own_first)
    width = pert_ref.shape[2] // tiles
    levs = pert_ref.shape[0]
    step = 16
    turn_shape = (step * levs, step * levs)
    turn_row = lax.broadcasted_iota(jnp.int32, turn_shape, 0)
    source = turn_row % levs * step + turn_row // levs
    turn = jnp.where(lax.broadcasted_iota(jnp.int32, turn_shape, 1) == source, 1.0, 0.0).astype(BF16)
    for pair in range(tiles // 2):
        news = [[] for _ in range(levs)]
        for side in range(2):
            left = jnp.concatenate(
                [new_ref[pair, :, part * LANES : part * LANES + members] for part in (side, side + 2)], axis=0
            )
            at = slice((pair * 2 + side) * width, (pair * 2 + side + 1) * width)
            pert = jnp.concatenate([pert_ref[lev, :, at] for lev in range(levs)], axis=1)
            both = jnp.dot(left, pert, preferred_element_type=F32)
            whole = both[:DROWS] + both[DROWS:]
            for lev in range(levs):
                new = whole[:, lev * width : (lev + 1) * width]
                gain = new[members : members + 1] + new[members + 1 : members + 2]
                out_mean_ref[lev : lev + 1, at] = mean_ref[lev : lev + 1, at] + gain / root
                news[lev].append(new[:members].astype(BF16))
        news = [jnp.concatenate(sides, axis=1) for sides in news]
        at = slice(pair * 2 * width, (pair + 1) * 2 * width)
        for start in range(0, members, step):
            block = jnp.concatenate([new[start : start + step] for new in news], axis=0)
            turned = jnp.dot(turn, block, preferred_element_type=F32).astype(BF16)
            out_ref[start * levs : (start + step) * levs, at] = turned


def swap(x, axis, bit):
    return lax.ppermute(x, axis, [(i, i ^ bit) for i in range(lax.axis_size(axis))])


def upper_bits(axis, first):
    bit, bits = first, []
    while bit < lax.axis_size(axis):
        bits.append(bit)
        bit *= 2
    return bits


def after(x, *others):
    return lax.optimization_barrier((x, *others))[0]


def body(perturbations, background, obs_cols, obs_levs, obs_vals, obs_sigma, pairs):
    members, lev_dev, col_dev = perturbations.shape
    batches, obs_own = obs_cols.shape
    tiles_dev, block_count = pairs.shape[1:]
    cols_size, owners = lax.axis_size("cols"), lax.axis_size("owner")
    tiles = tiles_dev * cols_size
    half = obs_own // 2
    blocks = half // LANES
    assert block_count // owners // 2 == blocks == 2
    assert col_dev == tiles_dev * LANES == LANES * LANES // block_count

    flat = perturbations.reshape(members * lev_dev, col_dev)
    rows = members + GROUP
    observed_scratch = [pltpu.VMEM((rows, obs_own), F32), pltpu.VMEM((col_dev, obs_own), BF16)]
    message = jax.ShapeDtypeStruct((members + batches * cols_size + blocks * rows, LANES), F32)
    sources = (flat, background, obs_cols, obs_levs, obs_sigma, obs_vals, pairs)
    keep, send = pl.pallas_call(
        first_kernel,
        in_specs=[pl.BlockSpec(memory_space=pltpu.MemorySpace.HBM)] * len(sources),
        out_shape=(message, message),
        scratch_shapes=fetch_scratch(sources, members) + observed_scratch,
        compiler_params=params(WHOLE_VMEM),
        name="first",
    )(*sources)

    def observe(which, obs_cols):
        shape = jax.ShapeDtypeStruct((blocks * len(which), rows, LANES), F32)
        return pl.pallas_call(
            functools.partial(observe_kernel, which),
            out_shape=(shape, shape),
            scratch_shapes=observed_scratch,
            compiler_params=params(),
            cost_estimate=pl.CostEstimate(flops=2 * 10**9 * len(which), bytes_accessed=10**7, transcendentals=0),
            name="observe",
        )(flat, background, obs_cols, obs_levs)

    stages = [("cols", bit) for bit in upper_bits("cols", 2)] + [("levs", bit) for bit in upper_bits("levs", 1)]
    total = keep + swap(send, "cols", 1)
    for axis, bit in stages:
        total = total + swap(total, axis, bit)
    gram_own = total[:members]

    def spread(gram_own):
        own = jnp.stack([gram_own] + [swap(gram_own, "owner", hop) for hop in range(1, owners)])
        return own, swap(own, "cols", 1)

    product = None
    for index in range(batches - 1):
        if index == 0:
            y_keep, y_send = observe(tuple(range(2, batches)), after(obs_cols, gram_own))
        own, peer = spread(gram_own)
        if index == 0:
            own = after(own, y_keep)
            y_later = y_keep + swap(y_send, "cols", 1)
            for axis, bit in stages:
                y_later = y_later + swap(y_later, axis, bit)
        if index == 1:
            by_level = jnp.transpose(after(perturbations, gram_own), (1, 0, 2))
            own = after(own, by_level)
        product, gram_own = pl.pallas_call(
            functools.partial(batch_kernel, index),
            out_shape=(
                jax.ShapeDtypeStruct((tiles // 2, DROWS, (4 if index else 2) * LANES), BF16),
                jax.ShapeDtypeStruct((members, LANES), F32),
            ),
            scratch_shapes=[pltpu.VMEM((2 * LANES, half), BF16), *factor_scratch(members, block_count, CHUNK)],
            compiler_params=params(),
            cost_estimate=pl.CostEstimate(flops=10**10, bytes_accessed=10**7, transcendentals=0),
            name="batch",
        )(total, own, peer, *((product, y_later) if index else ()), obs_cols, obs_sigma, obs_vals)

    own, peer = spread(gram_own)
    pairs_of = tiles_dev // 2
    mean, out = pl.pallas_call(
        functools.partial(last_kernel, batches),
        out_shape=(
            jax.ShapeDtypeStruct(background.shape, F32),
            jax.ShapeDtypeStruct(flat.shape, BF16),
        ),
        scratch_shapes=[
            pltpu.VMEM((pairs_of, DROWS, 4 * LANES), BF16),
            *factor_scratch(members, block_count, tiles_dev),
        ],
        compiler_params=params(),
        name="last",
    )(total, own, peer, product, by_level, background)
    return mean, out.reshape(perturbations.shape)


def solution(mesh):
    return jax.shard_map(
        body,
        mesh=mesh,
        in_specs=(
            P(None, "levs", "cols"),
            P("levs", "cols"),
            P(None, "owner"),
            P(None, "owner"),
            P(None, "owner"),
            P(None, "owner"),
            P(None, "cols", None),
        ),
        out_specs=(P("levs", "cols"), P(None, "levs", "cols")),
        check_vma=False,
    )
```

```python
import functools
import math

import jax
import jax.numpy as jnp
from jax import lax
from jax.experimental import pallas as pl
from jax.experimental.pallas import tpu as pltpu
from jax.sharding import PartitionSpec as P

F32 = jnp.float32
BF16 = jnp.bfloat16
LANES = 128
GROUP = 8
CHUNK = 32
DROWS = 96
VMEM_BYTES = 40 << 20
WHOLE_VMEM = 63 << 20


def params(limit=VMEM_BYTES):
    return pltpu.CompilerParams(vmem_limit_bytes=limit)


def split2(x):
    high = x.astype(BF16)
    return high, (x - high.astype(F32)).astype(BF16)


def nt_dot(a, b):
    return lax.dot_general(a, b, (((1,), (1,)), ((), ())), preferred_element_type=F32)


def observe_into(y_ref, hot_ref, pert_ref, mean_ref, local_cols, local_levs, ready=None):
    col_dev, count = hot_ref.shape
    lev_dev = mean_ref.shape[0]
    members = pert_ref.shape[0] // lev_dev
    for start in range(0, col_dev, 256):
        rows = lax.broadcasted_iota(jnp.int32, (256, count), 0) + start
        hot_ref[start : start + 256, :] = jnp.where(rows == local_cols, 1.0, 0.0).astype(BF16)
    lev_hot = lax.broadcasted_iota(jnp.int32, (lev_dev, count), 0) == local_levs
    hot = hot_ref[...]
    step = 16
    for start in range(0, members, step):
        if ready is not None:
            ready(start // step)
        picked = jnp.dot(
            pert_ref[start * lev_dev : (start + step) * lev_dev, :], hot, preferred_element_type=F32
        ).reshape(step, lev_dev, count)
        y_ref[start : start + step, :] = jnp.sum(jnp.where(lev_hot[None], picked, 0.0), axis=1)
    mean = mean_ref[...]
    high = mean.astype(BF16)
    rest = mean - high.astype(F32)
    middle = rest.astype(BF16)
    low = (rest - middle.astype(F32)).astype(BF16)
    picked = jnp.dot(jnp.concatenate([high, middle, low], axis=0), hot, preferred_element_type=F32)
    picked = (
        picked[:lev_dev] + picked[lev_dev : 2 * lev_dev] + picked[2 * lev_dev : 3 * lev_dev]
    )
    total = jnp.sum(jnp.where(lev_hot, picked, 0.0), axis=0, keepdims=True)
    tail = y_ref.shape[0] - members
    first = lax.broadcasted_iota(jnp.int32, (tail, count), 0) == 0
    y_ref[members:, :] = jnp.where(first, jnp.broadcast_to(total, (tail, count)), 0.0)


def half_first(x, core):
    half = x.shape[1] // 2
    return jnp.where(core == 0, x, jnp.concatenate([x[:, half:], x[:, :half]], axis=1))


def packed_grams(values, mean_row, sigma, vals, members):
    root = math.sqrt(members - 1.0)
    count = values.shape[1]
    scale = 1.0 / (sigma * root)
    innov = (vals - mean_row) / sigma
    wide = values.astype(F32) * (scale * scale)
    pad = LANES - members
    first = lax.broadcasted_iota(jnp.int32, (pad, count), 0) == 0
    last = jnp.where(first, jnp.broadcast_to(scale * innov, (pad, count)), 0.0)
    high, low = split2(jnp.concatenate([wide, last], axis=0))
    row = lax.broadcasted_iota(jnp.int32, (members, LANES), 0)
    lane = tile_lanes((members, LANES))
    results = []
    for start in range(0, count, 2 * LANES):
        grams = []
        for at in (slice(start, start + LANES), slice(start + LANES, start + 2 * LANES)):
            left = jnp.concatenate([values[:, at], values[:, at]], axis=1)
            right = jnp.concatenate([high[:, at], low[:, at]], axis=1)
            grams.append(nt_dot(left, right))
        a, b = grams
        diagonal = jnp.sum(jnp.where(lane == row, b, 0.0), axis=1, keepdims=True)
        packed = jnp.where((lane <= row) | (lane == members), a, jnp.where(lane < members, b, 0.0))
        packed = jnp.where(lane == members + 1, b[:, members : members + 1], packed)
        results.append(jnp.where(lane == members + 2, diagonal, packed))
    return results


def unpack_into(full_ref, refs, members):
    row = lax.broadcasted_iota(jnp.int32, (members, LANES), 0)
    lane = tile_lanes((members, LANES))
    index = 0
    for ref in refs:
        for block in range(ref.shape[0]):
            packed = ref[block]
            square = jnp.concatenate([packed, jnp.zeros((LANES - members, LANES), F32)], axis=0)
            turned = square.T[:members]
            full_ref[index] = jnp.where(
                (lane <= row) | (lane == members), packed, jnp.where(lane < members, turned, 0.0)
            )
            other = jnp.where(lane == row, packed[:, members + 2 : members + 3], jnp.where(lane < row, turned, packed))
            full_ref[index + 1] = jnp.where(
                lane < members, other, jnp.where(lane == members, packed[:, members + 1 : members + 2], 0.0)
            )
            index += 2


def observe_batch(y_ref, hot_ref, pert_ref, mean_ref, cols_ref, levs_ref, batch, ready=None):
    core = lax.axis_index("cols") % 2
    col_dev, lev_dev = hot_ref.shape[0], mean_ref.shape[0]
    cols = half_first(cols_ref[batch : batch + 1, :], core) - lax.axis_index("cols") * col_dev
    levs = half_first(levs_ref[batch : batch + 1, :], core) - lax.axis_index("levs") * lev_dev
    observe_into(y_ref, hot_ref, pert_ref, mean_ref, cols, levs, ready)


def store_blocks(y_ref, keep_refs, send_refs):
    for block, ref in enumerate((*keep_refs, *send_refs)):
        ref[...] = y_ref[:, block * LANES : (block + 1) * LANES]


def fetch(sources, held, sems, pert_sems):
    pert_ref, mean_ref = held[:2]
    small = [pltpu.make_async_copy(sources[i], held[i], sems.at[i - 1]) for i in range(1, len(held))]
    step = 16 * mean_ref.shape[0]
    large = [
        pltpu.make_async_copy(sources[0].at[start : start + step, :], pert_ref.at[start : start + step, :], pert_sems.at[i])
        for i, start in enumerate(range(0, pert_ref.shape[0], step))
    ]
    for copy in small + large:
        copy.start()
    for copy in small:
        copy.wait()
    return large


def fetch_scratch(sources, members):
    return [pltpu.VMEM(x.shape, x.dtype) for x in sources] + [
        pltpu.SemaphoreType.DMA((len(sources) - 1,)),
        pltpu.SemaphoreType.DMA((members // 16,)),
    ]


def first_kernel(*refs):
    sources, (keep_ref, send_ref), scratch = refs[:7], refs[7:9], refs[9:]
    held, (sems, pert_sems, y_ref, hot_ref) = scratch[:7], scratch[7:]
    pert_ref, mean_ref, cols_ref, levs_ref, sigma_ref, vals_ref, pair_ref = held
    large = fetch(sources, held, sems, pert_sems)
    core = lax.axis_index("cols") % 2
    members = pert_ref.shape[0] // mean_ref.shape[0]
    batches, tiles_dev, block_count = pair_ref.shape
    observe_batch(y_ref, hot_ref, pert_ref, mean_ref, cols_ref, levs_ref, 0, lambda i: large[i].wait())
    grams = packed_grams(
        y_ref[:members, :].astype(BF16),
        y_ref[members : members + 1, :],
        half_first(sigma_ref[0:1, :], core),
        half_first(vals_ref[0:1, :], core),
        members,
    )
    cols_size = lax.axis_size("cols")
    extra = batches * cols_size
    spread = jnp.where(
        tile_lanes((block_count, LANES)) % block_count == lax.broadcasted_iota(jnp.int32, (block_count, LANES), 0), 1.0, 0.0
    ).astype(BF16)
    mine = tile_lanes((tiles_dev, LANES)) // block_count == lax.broadcasted_iota(jnp.int32, (tiles_dev, LANES), 0)
    row = lax.broadcasted_iota(jnp.int32, (extra, LANES), 0)
    total = jnp.zeros((extra, LANES), F32)
    for batch in range(batches):
        wide = jnp.dot(pair_ref[batch].astype(F32).astype(BF16), spread, preferred_element_type=F32)
        line = jnp.sum(jnp.where(mine, wide, 0.0), axis=0, keepdims=True)
        total = jnp.where(row == batch * cols_size + lax.axis_index("cols"), line, total)
    total = jnp.where(lax.axis_index("levs") == 0, total, 0.0)
    for ref, gram in zip((keep_ref, send_ref), grams):
        ref[:members, :] = gram
        ref[members : members + extra, :] = total
    observe_batch(y_ref, hot_ref, pert_ref, mean_ref, cols_ref, levs_ref, 1)
    rows = y_ref.shape[0]
    places = range(members + extra, keep_ref.shape[0], rows)
    store_blocks(y_ref, *[[ref.at[place : place + rows, :] for place in places] for ref in (keep_ref, send_ref)])


def observe_kernel(batches, pert_ref, mean_ref, cols_ref, levs_ref, keep_ref, send_ref, y_ref, hot_ref):
    per = keep_ref.shape[0] // len(batches)
    for index, batch in enumerate(batches):
        observe_batch(y_ref, hot_ref, pert_ref, mean_ref, cols_ref, levs_ref, batch)
        store_blocks(y_ref, [keep_ref.at[index * per + i] for i in range(per)], [send_ref.at[index * per + i] for i in range(per)])


def tile_lanes(shape):
    return lax.broadcasted_iota(jnp.int32, shape, 1)


def block_order(block_count, own_blocks):
    place = lax.broadcasted_iota(jnp.int32, (2 * block_count * GROUP, LANES), 0) // GROUP % block_count
    side, rest = place // (block_count // 2), place % (block_count // 2)
    hop, block = rest // own_blocks, rest % own_blocks
    core = lax.axis_index("cols") % 2
    wanted = (lax.axis_index("owner") ^ hop) * (2 * own_blocks) + (core ^ side) * own_blocks + block
    return jnp.where(wanted == lax.broadcasted_iota(jnp.int32, wanted.shape, 1) % block_count, 1.0, 0.0).astype(BF16)


def pair_rows(lines, block_count):
    per = LANES // block_count
    rows = jnp.concatenate(
        [jnp.broadcast_to(lines[i : i + 1, :], (per, LANES)) for i in range(lines.shape[0])], axis=0
    )
    row = lax.broadcasted_iota(jnp.int32, rows.shape, 0)
    return jnp.where(tile_lanes(rows.shape) // block_count == row % per, rows, 0.0)


def build_systems(s_ref, pairs, full_ref):
    members = full_ref.shape[1]
    chunk = pairs.shape[0]
    pack = LANES // chunk
    order = block_order(full_ref.shape[0], 2)
    width = GROUP * chunk
    spread = nt_dot(order, jnp.concatenate([pairs.astype(BF16)] * (max(width, LANES) // chunk), axis=0))
    row = lax.broadcasted_iota(jnp.int32, spread.shape, 0)
    lane = tile_lanes(spread.shape)
    sides = max(1, LANES // width)
    select = jnp.concatenate(
        [jnp.where(row % GROUP + side * GROUP == lane // chunk, spread, 0.0) for side in range(sides)], axis=0
    ).astype(BF16)
    rows = s_ref.shape[1]
    out_row = lax.broadcasted_iota(jnp.int32, (rows, LANES), 0)
    out_pack = tile_lanes((rows, LANES)) // chunk
    for start in range(0, members, GROUP * sides):
        parts = []
        for side in range(sides):
            at = slice(start + side * GROUP, start + (side + 1) * GROUP)
            stacked = jnp.concatenate([full_ref[block, at, :] for block in range(full_ref.shape[0])], axis=0)
            parts.extend(split2(stacked.T[:rows]))
        product = jnp.dot(jnp.concatenate(parts, axis=1), select, preferred_element_type=F32)
        for part in range(product.shape[1] // LANES):
            first = start + part * pack
            s_ref[first // pack] = product[:, part * LANES : (part + 1) * LANES] + jnp.where(
                out_row == first + out_pack, 1.0, 0.0
            )


def invert_factors(s_ref, r_ref, m_ref, wrow_ref, members):
    one = jnp.where(
        lax.broadcasted_iota(jnp.int32, (LANES, LANES), 0) == tile_lanes((LANES, LANES)), 1.0, 0.0
    ).astype(BF16)
    pad = jnp.zeros((LANES - members, LANES), F32)
    rows = s_ref.shape[1]
    chunk = wrow_ref.shape[0]
    pack_size = LANES // chunk
    pack = tile_lanes((GROUP, LANES)) // chunk
    within = tile_lanes((rows, LANES)) % chunk
    group_row = lax.broadcasted_iota(jnp.int32, (GROUP, LANES), 0)
    count = members // GROUP
    weights = [jnp.zeros((GROUP, LANES), F32) for _ in range(count)]
    picks = [within + p * chunk for p in range(pack_size)]
    share = min(pack_size, GROUP)
    for s in range(count):
        start = s * GROUP
        first = start // pack_size
        inner = start % pack_size
        copies = []
        for a in range(GROUP):
            copies.append(jnp.take_along_axis(s_ref[first + a // share], picks[inner + a % share], axis=1))
        entry = [[None] * GROUP for _ in range(GROUP)]
        for a in range(GROUP):
            for b in range(a, GROUP):
                entry[a][b] = jnp.broadcast_to(copies[a][start + b : start + b + 1, :], (GROUP, LANES))
        ratio = [[None] * GROUP for _ in range(GROUP)]
        inverse = [None] * GROUP
        for a in range(GROUP):
            inverse[a] = pl.reciprocal(entry[a][a])
            for b in range(a + 1, GROUP):
                ratio[b][a] = entry[a][b] * inverse[a]
            for b in range(a + 1, GROUP):
                for c in range(b, GROUP):
                    entry[b][c] = entry[b][c] - ratio[b][a] * entry[a][c]
        roots = [lax.rsqrt(entry[a][a]) for a in range(GROUP)]
        pieces = rows // GROUP
        lower = [[None] * pieces for _ in range(GROUP)]
        for v in range(pieces):
            for a in range(GROUP):
                if v == s:
                    value = jnp.where(group_row == a, 1.0, 0.0)
                else:
                    value = copies[a][v * GROUP : (v + 1) * GROUP, :]
                for b in range(a):
                    value = value - ratio[a][b] * lower[b][v]
                lower[a][v] = value
        more = start + GROUP < members
        if more:
            for v in range(pieces):
                solved = [None] * GROUP
                for a in range(GROUP - 1, -1, -1):
                    value = lower[a][v] * inverse[a]
                    for b in range(a + 1, GROUP):
                        value = value - ratio[b][a] * solved[b]
                    solved[a] = value
                for a in range(GROUP):
                    value = solved[a]
                    if v == s:
                        value = value + jnp.where(group_row == a, 1.0, 0.0)
                    r_ref[s % 2 * GROUP + a, v * GROUP : (v + 1) * GROUP, :] = value
        for part in range(GROUP // share):

            def merged(v):
                value = lower[part * share][v] * roots[part * share]
                for p in range(1, share):
                    a = part * share + p
                    value = jnp.where(pack == inner + p, lower[a][v] * roots[a], value)
                return value

            halfway = jnp.broadcast_to(merged(count)[0:1, :], (GROUP, LANES))
            finished = [merged(v) for v in range(s + 1)]
            valid = (pack >= inner) & (pack < inner + share)
            for v in range(s + 1):
                weights[v] = weights[v] + jnp.where(valid, halfway * finished[v], 0.0)
            finished += [jnp.zeros((GROUP, LANES), F32)] * (count - 1 - s)
            block = first + part
            turned = nt_dot(one, jnp.concatenate(finished + [pad], axis=0).astype(BF16))
            at = inner * chunk
            m_ref[block * LANES + at : block * LANES + at + share * chunk, :] = turned[at : at + share * chunk]
        if more:

            def update(block, masked, start=start, inner=inner, side=s % 2 * GROUP):
                old = s_ref[block, start : start + GROUP, :]
                if masked:
                    old = jnp.where(pack >= inner + GROUP, old, 0.0)
                factors = [jnp.broadcast_to(old[a : a + 1, :], (GROUP, LANES)) for a in range(GROUP)]
                for v in range(pieces):
                    at = slice(v * GROUP, (v + 1) * GROUP)
                    value = s_ref[block, at, :]
                    for a in range(GROUP):
                        value = value - factors[a] * r_ref[side + a, at, :]
                    s_ref[block, at, :] = value

            if pack_size > GROUP:
                if inner + GROUP < pack_size:
                    update(first, True)
                for block in range(first + 1, s_ref.shape[0]):
                    update(block, False)
            else:
                per = GROUP // pack_size

                def trailing(index, carry, first=first, update=update, per=per):
                    for step in range(per):
                        update(first + (index + 1) * per + step, False)
                    return carry

                trips = count - 1 - s
                lax.fori_loop(0, trips, trailing, 0, unroll=trips if trips <= 6 else {7: 1, 8: 4}.get(trips, 3))
    for v in range(count):
        shift = chunk
        while shift < LANES:
            weights[v] = weights[v] + pltpu.roll(weights[v], shift, 1)
            shift *= 2
    wrow_ref[...] = nt_dot(one[:chunk], jnp.concatenate(weights + [pad], axis=0).astype(BF16))


def factor_chunk(pairs, s_ref, r_ref, m_ref, wrow_ref, full_ref):
    build_systems(s_ref, pairs, full_ref)
    invert_factors(s_ref, r_ref, m_ref, wrow_ref, full_ref.shape[1])


def factor_scratch(members, block_count, chunk):
    return [
        pltpu.VMEM((members * chunk // LANES, members + GROUP, LANES), F32),
        pltpu.VMEM((2 * GROUP, members + GROUP, LANES), F32),
        pltpu.VMEM((members * chunk, LANES), F32),
        pltpu.VMEM((chunk, LANES), F32),
        pltpu.VMEM((block_count, members, LANES), F32),
    ]


def product_of(m_ref, w_ref, tile, old, members):
    rows = m_ref[pl.ds(tile, members, stride=w_ref.shape[0]), :].astype(BF16)
    tail = DROWS - members
    sub = lax.broadcasted_iota(jnp.int32, (tail, LANES), 0)
    lane = lax.broadcasted_iota(jnp.int32, (tail, LANES), 1)
    weights = jnp.broadcast_to(w_ref[pl.ds(tile, 1), :], (tail, LANES))
    if old is None:
        return jnp.concatenate([rows, jnp.where(sub == 0, weights, 0.0).astype(BF16)], axis=0), None
    ones = (lane >= members) & (lane < members + 2)
    extra = jnp.where(sub == 0, jnp.where(ones, 1.0, weights), 0.0).astype(BF16)
    left = jnp.concatenate([rows, extra], axis=0)[:, :DROWS]
    new = jnp.dot(left, old[0], preferred_element_type=F32)
    if old[1] is not None:
        new = new + jnp.dot(left, old[1], preferred_element_type=F32)
    total = jnp.broadcast_to(new[members : members + 1, :], (tail, LANES))
    high = total.astype(BF16).astype(F32)
    last = jnp.where(sub == 0, high, jnp.where(sub == 1, total - high, 0.0))
    return split2(jnp.concatenate([new[:members], last], axis=0))


def products(m_ref, w_ref, old_ref, new_ref, base, pairs_of, members, old_base=None):
    old_base = base if old_base is None else old_base

    def pair(index, carry):
        for side in range(2):
            at = slice(side * LANES, (side + 1) * LANES)
            low_at = slice((side + 2) * LANES, (side + 3) * LANES)
            old = None
            if old_ref is not None:
                old = old_ref[old_base + index, :, at], None
                if old_ref.shape[2] > 2 * LANES:
                    old = old[0], old_ref[old_base + index, :, low_at]
            high, low = product_of(m_ref, w_ref, index * 2 + side, old, members)
            new_ref[base + index, :, at] = high
            if low is not None:
                new_ref[base + index, :, low_at] = low
        return carry

    lax.fori_loop(0, pairs_of, pair, 0, unroll=4)


def factor_part(index, total_ref, own_ref, peer_ref, old_ref, new_ref, factor):
    members = own_ref.shape[1]
    block_count = factor[4].shape[0]
    cols_size = lax.axis_size("cols")
    unpack_into(factor[4], (own_ref, peer_ref), members)
    lines = CHUNK * block_count // LANES
    chunks = cols_size // lines

    def one_chunk(chunk):
        rows = total_ref[pl.ds(members + index * cols_size + chunk * lines, lines), :]
        factor_chunk(pair_rows(rows, block_count), *factor)
        products(factor[2], factor[3], old_ref, new_ref, chunk * (CHUNK // 2), CHUNK // 2, members)

    if chunks == 1:
        one_chunk(0)
    else:
        pl.loop(0, chunks)(one_chunk)


def moments_part(index, y, cols_ref, sigma_ref, vals_ref, new_ref, gram_ref, x_ref):
    members = gram_ref.shape[0]
    root = math.sqrt(members - 1.0)
    core = lax.axis_index("cols") % 2
    count = x_ref.shape[1]
    later = slice(index + 1, index + 2)
    tile = half_first(cols_ref[later, :], core)[:, :count] // LANES
    y = jnp.concatenate(y, axis=1)
    start_values = y[:members, :]
    empty = jnp.zeros((LANES - members, count), BF16)
    for side in range(2):
        x_ref[side * LANES : side * LANES + members, :] = jnp.where(tile % 2 == side, start_values, 0.0).astype(BF16)
        x_ref[side * LANES + members : (side + 1) * LANES, :] = empty
    parts = new_ref.shape[2] // (2 * LANES)
    stacked = jnp.concatenate([x_ref[...]] * parts, axis=0)
    half_tile = tile // 2
    per = 4

    def gather(index, total):
        at = new_ref[pl.ds(index * per, per)].reshape(per * DROWS, new_ref.shape[2])
        product = jnp.dot(at, stacked, preferred_element_type=F32)
        for k in range(per):
            total = jnp.where(half_tile == index * per + k, product[k * DROWS : (k + 1) * DROWS], total)
        return total

    now = lax.fori_loop(0, new_ref.shape[0] // per, gather, jnp.zeros((DROWS, count), F32), unroll=4)
    mean_row = y[members : members + 1, :] + (now[members : members + 1] + now[members + 1 : members + 2]) / root
    gram_ref[...] = packed_grams(
        now[:members].astype(BF16),
        mean_row,
        half_first(sigma_ref[later, :], core)[:, :count],
        half_first(vals_ref[later, :], core)[:, :count],
        members,
    )[0]


def batch_kernel(index, total_ref, own_ref, peer_ref, *refs):
    old_ref, y_ref = refs[:2] if index else (None, None)
    cols_ref, sigma_ref, vals_ref, new_ref, gram_ref, x_ref, *factor = refs[2 if index else 0 :]
    members = own_ref.shape[1]
    factor_part(index, total_ref, own_ref, peer_ref, old_ref, new_ref, factor)
    blocks = x_ref.shape[1] // LANES
    if index:
        y = [y_ref[(index - 1) * blocks + block] for block in range(blocks)]
    else:
        rows = members + GROUP
        places = range(total_ref.shape[0] - blocks * rows, total_ref.shape[0], rows)
        y = [total_ref[place : place + rows, :] for place in places]
    moments_part(index, y, cols_ref, sigma_ref, vals_ref, new_ref, gram_ref, x_ref)


def last_kernel(batches, total_ref, own_ref, peer_ref, old_ref, pert_ref, mean_ref, out_mean_ref, out_ref, new_ref, *factor):
    members = own_ref.shape[1]
    root = math.sqrt(members - 1.0)
    tiles = new_ref.shape[0] * 2
    unpack_into(factor[4], (own_ref, peer_ref), members)
    cols_size = lax.axis_size("cols")
    line = total_ref[pl.ds(members + (batches - 1) * cols_size + lax.axis_index("cols"), 1), :]
    pairs = pair_rows(line, factor[4].shape[0])
    factor_chunk(pairs, *factor)
    own_first = lax.axis_index("cols") * new_ref.shape[0]
    products(factor[2], factor[3], old_ref, new_ref, 0, new_ref.shape[0], members, own_first)
    width = pert_ref.shape[2] // tiles
    levs = pert_ref.shape[0]
    step = 16
    turn_shape = (step * levs, step * levs)
    turn_row = lax.broadcasted_iota(jnp.int32, turn_shape, 0)
    source = turn_row % levs * step + turn_row // levs
    turn = jnp.where(lax.broadcasted_iota(jnp.int32, turn_shape, 1) == source, 1.0, 0.0).astype(BF16)
    for pair in range(tiles // 2):
        news = [[] for _ in range(levs)]
        for side in range(2):
            left = jnp.concatenate(
                [new_ref[pair, :, part * LANES : part * LANES + members] for part in (side, side + 2)], axis=0
            )
            at = slice((pair * 2 + side) * width, (pair * 2 + side + 1) * width)
            pert = jnp.concatenate([pert_ref[lev, :, at] for lev in range(levs)], axis=1)
            both = jnp.dot(left, pert, preferred_element_type=F32)
            whole = both[:DROWS] + both[DROWS:]
            for lev in range(levs):
                new = whole[:, lev * width : (lev + 1) * width]
                gain = new[members : members + 1] + new[members + 1 : members + 2]
                out_mean_ref[lev : lev + 1, at] = mean_ref[lev : lev + 1, at] + gain / root
                news[lev].append(new[:members].astype(BF16))
        news = [jnp.concatenate(sides, axis=1) for sides in news]
        at = slice(pair * 2 * width, (pair + 1) * 2 * width)
        for start in range(0, members, step):
            block = jnp.concatenate([new[start : start + step] for new in news], axis=0)
            turned = jnp.dot(turn, block, preferred_element_type=F32).astype(BF16)
            out_ref[start * levs : (start + step) * levs, at] = turned


def swap(x, axis, bit):
    return lax.ppermute(x, axis, [(i, i ^ bit) for i in range(lax.axis_size(axis))])


def upper_bits(axis, first):
    bit, bits = first, []
    while bit < lax.axis_size(axis):
        bits.append(bit)
        bit *= 2
    return bits


def after(x, *others):
    return lax.optimization_barrier((x, *others))[0]


def body(perturbations, background, obs_cols, obs_levs, obs_vals, obs_sigma, pairs):
    members, lev_dev, col_dev = perturbations.shape
    batches, obs_own = obs_cols.shape
    tiles_dev, block_count = pairs.shape[1:]
    cols_size, owners = lax.axis_size("cols"), lax.axis_size("owner")
    tiles = tiles_dev * cols_size
    half = obs_own // 2
    blocks = half // LANES
    assert block_count // owners // 2 == blocks == 2
    assert col_dev == tiles_dev * LANES == LANES * LANES // block_count

    flat = perturbations.reshape(members * lev_dev, col_dev)
    rows = members + GROUP
    observed_scratch = [pltpu.VMEM((rows, obs_own), F32), pltpu.VMEM((col_dev, obs_own), BF16)]
    message = jax.ShapeDtypeStruct((members + batches * cols_size + blocks * rows, LANES), F32)
    sources = (flat, background, obs_cols, obs_levs, obs_sigma, obs_vals, pairs)
    keep, send = pl.pallas_call(
        first_kernel,
        in_specs=[pl.BlockSpec(memory_space=pltpu.MemorySpace.HBM)] * len(sources),
        out_shape=(message, message),
        scratch_shapes=fetch_scratch(sources, members) + observed_scratch,
        compiler_params=params(WHOLE_VMEM),
        name="first",
    )(*sources)

    def observe(which, obs_cols):
        shape = jax.ShapeDtypeStruct((blocks * len(which), rows, LANES), F32)
        return pl.pallas_call(
            functools.partial(observe_kernel, which),
            out_shape=(shape, shape),
            scratch_shapes=observed_scratch,
            compiler_params=params(),
            cost_estimate=pl.CostEstimate(flops=2 * 10**9 * len(which), bytes_accessed=10**7, transcendentals=0),
            name="observe",
        )(flat, background, obs_cols, obs_levs)

    stages = [("cols", bit) for bit in upper_bits("cols", 2)] + [("levs", bit) for bit in upper_bits("levs", 1)]
    total = keep + swap(send, "cols", 1)
    for axis, bit in stages:
        total = total + swap(total, axis, bit)
    gram_own = total[:members]

    def spread(gram_own):
        own = jnp.stack([gram_own] + [swap(gram_own, "owner", hop) for hop in range(1, owners)])
        return own, swap(own, "cols", 1)

    product = None
    for index in range(batches - 1):
        if index == 0:
            y_keep, y_send = observe(tuple(range(2, batches)), after(obs_cols, gram_own))
        own, peer = spread(gram_own)
        if index == 0:
            own = after(own, y_keep)
            y_later = y_keep + swap(y_send, "cols", 1)
            for axis, bit in stages:
                y_later = y_later + swap(y_later, axis, bit)
        if index == 1:
            by_level = jnp.transpose(after(perturbations, gram_own), (1, 0, 2))
            own = after(own, by_level)
        product, gram_own = pl.pallas_call(
            functools.partial(batch_kernel, index),
            out_shape=(
                jax.ShapeDtypeStruct((tiles // 2, DROWS, (4 if index else 2) * LANES), BF16),
                jax.ShapeDtypeStruct((members, LANES), F32),
            ),
            scratch_shapes=[pltpu.VMEM((2 * LANES, half), BF16), *factor_scratch(members, block_count, CHUNK)],
            compiler_params=params(),
            cost_estimate=pl.CostEstimate(flops=10**10, bytes_accessed=10**7, transcendentals=0),
            name="batch",
        )(total, own, peer, *((product, y_later) if index else ()), obs_cols, obs_sigma, obs_vals)

    own, peer = spread(gram_own)
    pairs_of = tiles_dev // 2
    mean, out = pl.pallas_call(
        functools.partial(last_kernel, batches),
        out_shape=(
            jax.ShapeDtypeStruct(background.shape, F32),
            jax.ShapeDtypeStruct(flat.shape, BF16),
        ),
        scratch_shapes=[
            pltpu.VMEM((pairs_of, DROWS, 4 * LANES), BF16),
            *factor_scratch(members, block_count, tiles_dev),
        ],
        compiler_params=params(),
        name="last",
    )(total, own, peer, product, by_level, background)
    return mean, out.reshape(perturbations.shape)


def solution(mesh):
    return jax.shard_map(
        body,
        mesh=mesh,
        in_specs=(
            P(None, "levs", "cols"),
            P("levs", "cols"),
            P(None, "owner"),
            P(None, "owner"),
            P(None, "owner"),
            P(None, "owner"),
            P(None, "cols", None),
        ),
        out_specs=(P("levs", "cols"), P(None, "levs", "cols")),
        check_vma=False,
    )
```
